32 devices in a mesh: groups: 2 (over x), seq: 16 (over z, y, core).
Axes of the slice: x: 2, y: 2, z: 4, core: 2. Of those that a mesh axis runs over, the one named last changes fastest.
Arguments:
- inputs: bfloat16 [4096, 2048], P(('groups', 'seq')), parts along dimension 0, may hold values from -0.015625 to 0.015625
- grad_out: bfloat16 [4096, 2048], P(('groups', 'seq')), parts along dimension 0, may hold values from -6 to 6
- filter_weight: float32 [32, 2048], replicated, may hold values from -0.0625 to 0.0625
- filter_rates: float32 [32], replicated, may hold values from 9.765625e-05 to 0.03
- filter_freqs: float32 [32], replicated, may hold values from 0 to 3
- skip_gain: float32 [2048], replicated, may hold values from 0.1 to 1.9
- span_of_slot: int32 [64], P('groups'), parts along dimension 0, may hold values from 0 to 31, as said below
Outputs:
- input_grad: bfloat16 [4096, 2048], P(('groups', 'seq')), parts along dimension 0
- filter_weight_grad: float32 [64, 2048], P('groups', 'seq'), parts along dimension 0
The draws below stay inside these ranges and needn't reach their ends.
There are 2 independent parts, one for each index of `groups`. The reference program is written for one: setup_inputs(seed, part) draws one part's arguments, and reference() takes and returns one part's arrays. A program takes and returns all parts, laid end to end along the dimension named above; an argument that names none is the same for every part. Nothing has to cross between parts.
Inputs may be any that keep to these rules, and one draw needn't show every extreme that they name: `span_of_slot`: each span number appears once; the two row blocks of one device (slots 2 i and 2 i + 1) hold spans c and 31 - c for some c, in either order.
All inputs are finite; a program needn't handle non-finite values.
Results may differ from the reference program's by a relative error of at most 0.001.
Values may be sent and summed in bfloat16 or wider, within the bound.
No kernel may reach another device: no remote copies, remote signals or barrier semaphores. Data moves between devices by JAX's collectives and lax.ppermute only.
A program may use at most 64 MiB of HBM per device.

```python
import math
import jax
import jax.numpy as jnp
from jax import lax

C = 2048
J = 32
TOK_DEV = 128
SPANS = 32
LENGTH = 2048
N_SEQ = 16


def draw_span_of_slot(key, part):
    first_key, second_key = jax.random.split(jax.random.fold_in(key, 7))
    lower = jax.random.permutation(first_key, SPANS // 2).astype(jnp.int32)
    upper = (SPANS - 1 - lower).astype(jnp.int32)
    flipped = jax.random.randint(second_key, (SPANS // 2,), 0, 2)
    leading = jnp.where(flipped == 1, upper, lower)
    trailing = jnp.where(flipped == 1, lower, upper)
    return jnp.stack([leading, trailing], axis=1).reshape(SPANS).astype(jnp.int32)


def spiked(drawn, rng, source, target, blocks, factor):
    owner, partner = [(jnp.arange(drawn.shape[axis_at]) // (drawn.shape[axis_at] // blocks)).reshape([-1 if axis == axis_at else 1 for axis in range(drawn.ndim)]) for axis_at in (source, target)]
    chosen = jax.random.permutation(rng, blocks)[partner]
    strong = (owner == chosen) | (owner == (partner + blocks // 2) % blocks)
    return jnp.where(strong, factor * drawn, drawn)


def steps_of(key, shape, shards, smallest, largest):
    loudness = 1.0
    for dim, parts in shards:
        steps = jax.random.uniform(jax.random.fold_in(jax.random.fold_in(key, 6), dim), (parts,), jnp.float32, smallest / len(shards), largest / len(shards))
        loudness = loudness * jnp.repeat(jnp.exp(steps), shape[dim] // parts).reshape((-1,) + (1,) * (len(shape) - 1 - dim))
    return loudness


def gaussian(own_key, extent, spread, limit, cuts=(), dtype=jnp.bfloat16):
    drawn = spread * jax.random.normal(own_key, extent, jnp.float32)
    if cuts:
        drawn = drawn * steps_of(own_key, extent, cuts, -0.22, 0.18)
    return jnp.clip(drawn, -limit, limit).astype(dtype)


def gaussian_with(own_key, extent, scale, reach, cuts, heavy, dtype=jnp.bfloat16):
    array = scale * jax.random.normal(own_key, extent, jnp.float32)
    if cuts:
        array = array * steps_of(own_key, extent, cuts, -0.22, 0.18)
    return jnp.clip(spiked(array, jax.random.fold_in(own_key, 3), *heavy), -reach, reach).astype(dtype)


def setup_inputs(seed: int = 0, part: int = 0) -> dict:
    keys = jax.random.split(jax.random.key(seed), 8)
    own_keys = jax.random.split(jax.random.fold_in(keys[7], part), 8)
    inputs = gaussian(own_keys[0], (LENGTH, C), (2.0 / (TOK_DEV * N_SEQ)), 0.015625, ((0, 16),))
    grad_out = gaussian_with(own_keys[1], (LENGTH, C), 1.0, 6.0, ((0, 16),), (0, 1, 16, 2.0))
    filter_weight = gaussian(keys[2], (J, C), (J * TOK_DEV * N_SEQ // 8) ** -0.5, 0.0625, (), jnp.float32)
    filter_rates = jnp.clip(jnp.exp(jax.random.uniform(keys[3], (J,), jnp.float32, math.log(9.765625145519152e-05), math.log(0.03))), 9.765625145519152e-05, 0.03)
    filter_freqs = jnp.clip(jax.random.uniform(keys[4], (J,), jnp.float32, 0.0, 3.0), 0.0, 3.0)
    skip_gain = jnp.clip(1.0 + 0.18 * jax.random.normal(keys[5], (C,), jnp.float32), 0.1, 1.9)
    span_of_slot = draw_span_of_slot(jax.random.fold_in(jax.random.fold_in(keys[7], part), 71), part)
    return {"inputs": inputs, "grad_out": grad_out, "filter_weight": filter_weight, "filter_rates": filter_rates, "filter_freqs": filter_freqs, "skip_gain": skip_gain, "span_of_slot": span_of_slot}


def reference(inputs, grad_out, filter_weight, filter_rates, filter_freqs, skip_gain, span_of_slot):
    length = TOK_DEV * N_SEQ
    half_rows = TOK_DEV // 2
    span_order = jnp.argsort(span_of_slot)
    x_seq = inputs.reshape(SPANS, half_rows, C)[span_order].reshape(length, C).astype(jnp.float32)
    g_seq = grad_out.reshape(SPANS, half_rows, C)[span_order].reshape(length, C).astype(jnp.float32)
    lag_steps = jnp.arange(length).astype(jnp.float32)[:, None]
    basis_rows = jnp.exp(-lag_steps * filter_rates[None, :]) * jnp.cos(lag_steps * filter_freqs[None, :])
    taps = jnp.dot(basis_rows, filter_weight, precision=lax.Precision.HIGHEST, preferred_element_type=jnp.float32)
    spectrum_len = 2 * length
    taps_spec = jnp.fft.rfft(taps, n=spectrum_len, axis=0)
    grad_spec = jnp.fft.rfft(g_seq, n=spectrum_len, axis=0)
    input_spec = jnp.fft.rfft(x_seq, n=spectrum_len, axis=0)
    input_seq = jnp.fft.irfft(jnp.conj(taps_spec) * grad_spec, n=spectrum_len, axis=0)[:length]
    input_seq = input_seq + skip_gain[None, :] * g_seq
    tap_grads = jnp.fft.irfft(jnp.conj(input_spec) * grad_spec, n=spectrum_len, axis=0)[:length]
    weight_grad = jnp.dot(basis_rows.T, tap_grads, precision=lax.Precision.HIGHEST, preferred_element_type=jnp.float32)
    input_grad = input_seq.reshape(SPANS, half_rows, C)[span_of_slot].reshape(length, C).astype(jnp.bfloat16)
    return input_grad, weight_grad
```

```python
import functools
import math

import jax
import jax.numpy as jnp
import numpy as np
from jax import lax
from jax.experimental import pallas as pl
from jax.experimental.pallas import tpu as pltpu
from jax.sharding import PartitionSpec as P

HIGHEST = lax.Precision.HIGHEST
F32 = jnp.float32
BF16 = jnp.bfloat16
LANES = 128


def halves(value):
    high = value.astype(BF16)
    return high, (value - high.astype(F32)).astype(BF16)


def table_halves(value):
    high = lax.reduce_precision(value, 8, 7)
    return high.astype(BF16), (value - high).astype(BF16)


def odd_frequencies(rows):
    angles = np.pi * np.outer(2 * np.arange(rows) + 1, np.arange(rows)) / (2 * rows)
    return np.cos(angles), -np.sin(angles)


def tables(rows, rates, freqs):
    cos_part, sin_part = odd_frequencies(rows)
    forward = jnp.asarray(np.concatenate([cos_part, sin_part], 0), F32)
    inverse = jnp.asarray(np.concatenate([cos_part, sin_part], 0).T / rows, F32)
    lags = jnp.arange(rows + 1).astype(F32)[None, :]
    decay = jnp.exp(-lags * rates[:, None])
    power_real = decay * jnp.cos(lags * freqs[:, None])
    power_imag = decay * jnp.sin(lags * freqs[:, None])
    to_start = jnp.concatenate([power_real[:, :rows], power_imag[:, :rows]], 0)
    to_end = jnp.concatenate([power_real[:, :0:-1], power_imag[:, :0:-1]], 0)
    left_g = jnp.concatenate(table_halves(jnp.concatenate([forward, to_start], 0)), 1)
    left_x = jnp.concatenate(table_halves(jnp.concatenate([forward, to_end], 0)), 1)
    back = jnp.concatenate(
        [inverse, power_real[:, :0:-1].T, -power_imag[:, :0:-1].T], 1
    )
    back_high, back_low = table_halves(back)
    basis_spectrum = jnp.dot(
        forward, power_real[:, :rows].T, precision=HIGHEST, preferred_element_type=F32
    )
    step = jnp.stack([power_real[:, rows], power_imag[:, rows]], 0)[:, :, None]
    return left_g, left_x, back_high, back_low, basis_spectrum, step


def kernel(
    spans_ref,
    gx_ref,
    weight_ref,
    gain_ref,
    left_g_ref,
    left_x_ref,
    back_high_ref,
    back_low_ref,
    spectrum_ref,
    step_ref,
    y_ref,
    wgrad_ref,
    slot_of,
    sums_g,
    sums_x,
    high,
    low,
):
    n_src, _, rows_dev, width = gx_ref.shape
    rows = rows_dev // 2
    n_basis = weight_ref.shape[0]
    n_spans = 2 * n_src

    def invert(slot, carry):
        slot_of[spans_ref[slot]] = slot
        return carry

    lax.fori_loop(0, n_spans, invert, 0)
    weight = weight_ref[...]
    spectrum = spectrum_ref[...]
    taps = jnp.dot(spectrum, weight, precision=HIGHEST, preferred_element_type=F32)
    taps_real, taps_imag = taps[:rows], taps[rows:]

    def pair(source, which):
        first = gx_ref[source, which, :rows, :]
        second = gx_ref[source, which, rows:, :]
        both = jnp.concatenate([first, second], 1)
        return jnp.concatenate([both, both], 0)

    def analyse(source, carry):
        cross_real, cross_imag = carry
        of_g = jnp.dot(left_g_ref[...], pair(source, 0), preferred_element_type=F32)
        of_x = jnp.dot(left_x_ref[...], pair(source, 1), preferred_element_type=F32)
        for half in range(2):
            at = slice(half * width, (half + 1) * width)
            slot = 2 * source + half
            sums_g[slot] = of_g[2 * rows :, at]
            sums_x[slot] = of_x[2 * rows :, at]
            g_real, g_imag = of_g[:rows, at], of_g[rows : 2 * rows, at]
            x_real, x_imag = of_x[:rows, at], of_x[rows : 2 * rows, at]
            cross_real = cross_real + (x_real * g_real + x_imag * g_imag)
            cross_imag = cross_imag + (x_real * g_imag - x_imag * g_real)
            y_real = halves(taps_real * g_real + taps_imag * g_imag)
            y_imag = halves(taps_real * g_imag - taps_imag * g_real)
            high[slot, :rows] = y_real[0]
            high[slot, rows : 2 * rows] = y_imag[0]
            low[slot, :rows] = y_real[1]
            low[slot, rows : 2 * rows] = y_imag[1]
        return cross_real, cross_imag

    zero = jnp.zeros((rows, width), F32)
    cross_real, cross_imag = lax.fori_loop(0, n_src, analyse, (zero, zero))
    near = lax.dot_general(
        spectrum,
        jnp.concatenate([cross_real, cross_imag], 0) * (1.0 / rows),
        (((0,), (0,)), ((), ())),
        precision=HIGHEST,
        preferred_element_type=F32,
    )
    step_real = jnp.broadcast_to(step_ref[0], (n_basis, width))
    step_imag = jnp.broadcast_to(step_ref[1], (n_basis, width))

    def descend(index, carry):
        state_real, state_imag, total = carry
        slot = slot_of[n_spans - 1 - index]
        total = total + (
            state_real * sums_x[slot, :n_basis] - state_imag * sums_x[slot, n_basis:]
        )
        far_real, far_imag = halves(weight * state_real), halves(weight * state_imag)
        high[slot, 2 * rows : 2 * rows + n_basis] = far_real[0]
        high[slot, 2 * rows + n_basis :] = far_imag[0]
        low[slot, 2 * rows : 2 * rows + n_basis] = far_real[1]
        low[slot, 2 * rows + n_basis :] = far_imag[1]
        next_real = sums_g[slot, :n_basis] + step_real * state_real - step_imag * state_imag
        next_imag = sums_g[slot, n_basis:] + step_real * state_imag + step_imag * state_real
        return next_real, next_imag, total

    empty = jnp.zeros((n_basis, width), F32)
    total = lax.fori_loop(0, n_spans, descend, (empty, empty, near))[2]
    wgrad_ref[...] = total
    gain = gain_ref[...]

    def restore(source, carry):
        both_high = jnp.concatenate([high[2 * source], high[2 * source + 1]], 1)
        both_low = jnp.concatenate([low[2 * source], low[2 * source + 1]], 1)
        value = (
            jnp.dot(back_high_ref[...], both_high, preferred_element_type=F32)
            + jnp.dot(back_high_ref[...], both_low, preferred_element_type=F32)
            + jnp.dot(back_low_ref[...], both_high, preferred_element_type=F32)
        )
        for half in range(2):
            at = slice(half * rows, (half + 1) * rows)
            own = gx_ref[source, 0, at, :].astype(F32)
            y_ref[source, at, :] = (
                value[:, half * width : (half + 1) * width] + gain * own
            ).astype(BF16)
        return carry

    lax.fori_loop(0, n_src, restore, 0)


def on_device(inputs, grad_out, filter_weight, filter_rates, filter_freqs, skip_gain, span_of_slot):
    rows_dev, channels = inputs.shape
    rows = rows_dev // 2
    n_basis = filter_weight.shape[0]
    devices = lax.axis_size("seq")
    position = lax.axis_index("seq")
    own = channels // devices
    width = -(-own // LANES) * LANES
    widen = ((0, 0), (0, width - own))
    both = jnp.stack([grad_out, inputs], 0).reshape(2, rows_dev, devices, own)
    gx = lax.all_to_all(both.transpose(2, 0, 1, 3), "seq", 0, 0, tiled=True)
    gx = jnp.pad(gx, ((0, 0), (0, 0)) + widen)
    weight = jnp.pad(lax.dynamic_slice_in_dim(filter_weight, position * own, own, 1), widen)
    gain = jnp.pad(lax.dynamic_slice_in_dim(skip_gain[None, :], position * own, own, 1), widen)
    n_spans = 2 * devices
    vmem = pl.BlockSpec(memory_space=pltpu.VMEM)
    y, wgrad = pl.pallas_call(
        kernel,
        out_shape=(
            jax.ShapeDtypeStruct((devices, rows_dev, width), BF16),
            jax.ShapeDtypeStruct((n_basis, width), F32),
        ),
        in_specs=[pl.BlockSpec(memory_space=pltpu.SMEM)] + [vmem] * 9,
        out_specs=(vmem, vmem),
        scratch_shapes=[
            pltpu.SMEM((n_spans,), jnp.int32),
            pltpu.VMEM((n_spans, 2 * n_basis, width), F32),
            pltpu.VMEM((n_spans, 2 * n_basis, width), F32),
            pltpu.VMEM((n_spans, 2 * rows + 2 * n_basis, width), BF16),
            pltpu.VMEM((n_spans, 2 * rows + 2 * n_basis, width), BF16),
        ],
        name="spans",
    )(span_of_slot, gx, weight, gain, *tables(rows, filter_rates, filter_freqs))
    y = lax.all_to_all(y[:, :, :own], "seq", 0, 0, tiled=True)
    input_grad = y.transpose(1, 0, 2).reshape(rows_dev, channels)
    return input_grad, wgrad[:, :own]


def solution(mesh):
    placed = (
        P(("groups", "seq"), None),
        P(("groups", "seq"), None),
        P(),
        P(),
        P(),
        P(),
        P("groups"),
    )
    return jax.shard_map(
        on_device,
        mesh=mesh,
        in_specs=placed,
        out_specs=(P(("groups", "seq"), None), P("groups", "seq")),
        check_vma=False,
    )
```

```python
import functools
import math

import jax
import jax.numpy as jnp
import numpy as np
from jax import lax
from jax.experimental import pallas as pl
from jax.experimental.pallas import tpu as pltpu
from jax.sharding import PartitionSpec as P

HIGHEST = lax.Precision.HIGHEST
F32 = jnp.float32
BF16 = jnp.bfloat16
LANES = 128


def halves(value):
    high = value.astype(BF16)
    return high, (value - high.astype(F32)).astype(BF16)


def table_halves(value):
    high = lax.reduce_precision(value, 8, 7)
    return high.astype(BF16), (value - high).astype(BF16)


def odd_frequencies(rows):
    angles = np.pi * np.outer(2 * np.arange(rows) + 1, np.arange(rows)) / (2 * rows)
    return np.cos(angles), -np.sin(angles)


def tables(rows, rates, freqs):
    cos_part, sin_part = odd_frequencies(rows)
    forward = jnp.asarray(np.concatenate([cos_part, sin_part], 0), F32)
    inverse = jnp.asarray(np.concatenate([cos_part, sin_part], 0).T / rows, F32)
    lags = jnp.arange(rows + 1).astype(F32)[None, :]
    decay = jnp.exp(-lags * rates[:, None])
    power_real = decay * jnp.cos(lags * freqs[:, None])
    power_imag = decay * jnp.sin(lags * freqs[:, None])
    to_start = jnp.concatenate([power_real[:, :rows], power_imag[:, :rows]], 0)
    to_end = jnp.concatenate([power_real[:, :0:-1], power_imag[:, :0:-1]], 0)
    left_g = jnp.concatenate(table_halves(jnp.concatenate([forward, to_start], 0)), 1)
    left_x = jnp.concatenate(table_halves(jnp.concatenate([forward, to_end], 0)), 1)
    back = jnp.concatenate(
        [inverse, power_real[:, :0:-1].T, -power_imag[:, :0:-1].T], 1
    )
    back_high, back_low = table_halves(back)
    basis_spectrum = jnp.dot(
        forward, power_real[:, :rows].T, precision=HIGHEST, preferred_element_type=F32
    )
    step = jnp.stack([power_real[:, rows], power_imag[:, rows]], 0)[:, :, None]
    return left_g, left_x, back_high, back_low, basis_spectrum, step


def pair(gx_ref, source, which):
    rows = gx_ref.shape[2] // 2
    first = gx_ref[source, which, :rows, :]
    second = gx_ref[source, which, rows:, :]
    both = jnp.concatenate([first, second], 1)
    return jnp.concatenate([both, both], 0)


def fill_slots(spans_ref, slot_of):
    for slot in range(slot_of.shape[0]):
        slot_of[spans_ref[slot]] = slot


def step_rows(step_ref, width):
    return (
        jnp.broadcast_to(step_ref[0], (step_ref.shape[1], width)),
        jnp.broadcast_to(step_ref[1], (step_ref.shape[1], width)),
    )


def input_kernel(
    spans_ref,
    gx_ref,
    weight_ref,
    gain_ref,
    left_g_ref,
    back_high_ref,
    back_low_ref,
    spectrum_ref,
    step_ref,
    y_ref,
    states_ref,
    slot_of,
    sums,
    high,
    low,
):
    n_src, _, rows_dev, width = gx_ref.shape
    rows = rows_dev // 2
    n_basis = weight_ref.shape[0]
    n_spans = 2 * n_src
    fill_slots(spans_ref, slot_of)
    weight = weight_ref[...]
    taps = jnp.dot(spectrum_ref[...], weight, precision=HIGHEST, preferred_element_type=F32)
    taps_real, taps_imag = taps[:rows], taps[rows:]
    left = left_g_ref[...]
    for source in range(n_src):
        of_g = jnp.dot(left, pair(gx_ref, source, 0), preferred_element_type=F32)
        for half in range(2):
            at = slice(half * width, (half + 1) * width)
            slot = 2 * source + half
            sums[slot] = of_g[2 * rows :, at]
            g_real, g_imag = of_g[:rows, at], of_g[rows : 2 * rows, at]
            y_real = halves(taps_real * g_real + taps_imag * g_imag)
            y_imag = halves(taps_real * g_imag - taps_imag * g_real)
            high[slot, :rows] = y_real[0]
            high[slot, rows : 2 * rows] = y_imag[0]
            low[slot, :rows] = y_real[1]
            low[slot, rows : 2 * rows] = y_imag[1]
    step_real, step_imag = step_rows(step_ref, width)
    state_real = jnp.zeros((n_basis, width), F32)
    state_imag = jnp.zeros((n_basis, width), F32)
    for span in range(n_spans - 1, -1, -1):
        slot = slot_of[span]
        states_ref[slot, :n_basis] = state_real
        states_ref[slot, n_basis:] = state_imag
        far_real, far_imag = halves(weight * state_real), halves(weight * state_imag)
        high[slot, 2 * rows : 2 * rows + n_basis] = far_real[0]
        high[slot, 2 * rows + n_basis :] = far_imag[0]
        low[slot, 2 * rows : 2 * rows + n_basis] = far_real[1]
        low[slot, 2 * rows + n_basis :] = far_imag[1]
        next_real = sums[slot, :n_basis] + step_real * state_real - step_imag * state_imag
        state_imag = sums[slot, n_basis:] + step_real * state_imag + step_imag * state_real
        state_real = next_real
    gain = gain_ref[...]
    back_high, back_low = back_high_ref[...], back_low_ref[...]
    for source in range(n_src):
        both_high = jnp.concatenate([high[2 * source], high[2 * source + 1]], 1)
        both_low = jnp.concatenate([low[2 * source], low[2 * source + 1]], 1)
        value = (
            jnp.dot(back_high, both_high, preferred_element_type=F32)
            + jnp.dot(back_high, both_low, preferred_element_type=F32)
            + jnp.dot(back_low, both_high, preferred_element_type=F32)
        )
        for half in range(2):
            at = slice(half * rows, (half + 1) * rows)
            own = gx_ref[source, 0, at, :].astype(F32)
            y_ref[source, at, :] = (
                value[:, half * width : (half + 1) * width] + gain * own
            ).astype(BF16)


def weight_kernel(
    gx_ref, states_ref, left_g_ref, left_x_ref, spectrum_ref, wgrad_ref
):
    n_src, _, rows_dev, width = gx_ref.shape
    rows = rows_dev // 2
    n_basis = wgrad_ref.shape[0]

    def analyse(source, carry):
        cross_real, cross_imag, total = carry
        of_g = jnp.dot(
            left_g_ref[: 2 * rows], pair(gx_ref, source, 0), preferred_element_type=F32
        )
        of_x = jnp.dot(left_x_ref[...], pair(gx_ref, source, 1), preferred_element_type=F32)
        for half in range(2):
            at = slice(half * width, (half + 1) * width)
            slot = 2 * source + half
            g_real, g_imag = of_g[:rows, at], of_g[rows : 2 * rows, at]
            x_real, x_imag = of_x[:rows, at], of_x[rows : 2 * rows, at]
            sum_real = of_x[2 * rows : 2 * rows + n_basis, at]
            sum_imag = of_x[2 * rows + n_basis :, at]
            cross_real = cross_real + (x_real * g_real + x_imag * g_imag)
            cross_imag = cross_imag + (x_real * g_imag - x_imag * g_real)
            total = total + (
                states_ref[slot, :n_basis] * sum_real - states_ref[slot, n_basis:] * sum_imag
            )
        return cross_real, cross_imag, total

    zero = jnp.zeros((rows, width), F32)
    empty = jnp.zeros((n_basis, width), F32)
    cross_real, cross_imag, total = lax.fori_loop(0, n_src, analyse, (zero, zero, empty))
    near = lax.dot_general(
        spectrum_ref[...],
        jnp.concatenate([cross_real, cross_imag], 0) * (1.0 / rows),
        (((0,), (0,)), ((), ())),
        precision=HIGHEST,
        preferred_element_type=F32,
    )
    wgrad_ref[...] = total + near


def on_device(inputs, grad_out, filter_weight, filter_rates, filter_freqs, skip_gain, span_of_slot):
    rows_dev, channels = inputs.shape
    rows = rows_dev // 2
    n_basis = filter_weight.shape[0]
    devices = lax.axis_size("seq")
    position = lax.axis_index("seq")
    own = channels // devices
    width = -(-own // LANES) * LANES
    widen = ((0, 0), (0, width - own))
    gx = lax.all_to_all(
        jnp.concatenate([grad_out, inputs], 0), "seq", 1, 0, tiled=True
    ).reshape(devices, 2, rows_dev, own)
    gx = jnp.pad(gx, ((0, 0), (0, 0)) + widen)
    weight = jnp.pad(lax.dynamic_slice_in_dim(filter_weight, position * own, own, 1), widen)
    gain = jnp.pad(lax.dynamic_slice_in_dim(skip_gain[None, :], position * own, own, 1), widen)
    left_g, left_x, back_high, back_low, spectrum, step = tables(
        rows, filter_rates, filter_freqs
    )
    n_spans = 2 * devices
    depth = 2 * rows + 2 * n_basis
    vmem = pl.BlockSpec(memory_space=pltpu.VMEM)
    y, states = pl.pallas_call(
        input_kernel,
        out_shape=(
            jax.ShapeDtypeStruct((devices, rows_dev, width), BF16),
            jax.ShapeDtypeStruct((n_spans, 2 * n_basis, width), F32),
        ),
        in_specs=[pl.BlockSpec(memory_space=pltpu.SMEM)] + [vmem] * 8,
        out_specs=(vmem, vmem),
        scratch_shapes=[
            pltpu.SMEM((n_spans,), jnp.int32),
            pltpu.VMEM((n_spans, 2 * n_basis, width), F32),
            pltpu.VMEM((n_spans, depth, width), BF16),
            pltpu.VMEM((n_spans, depth, width), BF16),
        ],
        name="input_part",
    )(span_of_slot, gx, weight, gain, left_g, back_high, back_low, spectrum, step)
    y = y[:, :, :own].reshape(devices * rows_dev, own)
    input_grad = lax.all_to_all(y, "seq", 0, 1, tiled=True)
    wgrad = pl.pallas_call(
        weight_kernel,
        out_shape=jax.ShapeDtypeStruct((n_basis, width), F32),
        in_specs=[vmem] * 5,
        out_specs=vmem,
        cost_estimate=pl.CostEstimate(
            flops=2 * 2 * depth * rows_dev * n_spans * width,
            bytes_accessed=4 * n_spans * rows_dev * width,
            transcendentals=0,
        ),
        name="weight_part",
    )(gx, states, left_g, left_x, spectrum)
    return input_grad, wgrad[:, :own]


def solution(mesh):
    placed = (
        P(("groups", "seq"), None),
        P(("groups", "seq"), None),
        P(),
        P(),
        P(),
        P(),
        P("groups"),
    )
    return jax.shard_map(
        on_device,
        mesh=mesh,
        in_specs=placed,
        out_specs=(P(("groups", "seq"), None), P("groups", "seq")),
        check_vma=False,
    )
```

```python
import functools
import math

import jax
import jax.numpy as jnp
import numpy as np
from jax import lax
from jax.experimental import pallas as pl
from jax.experimental.pallas import tpu as pltpu
from jax.sharding import PartitionSpec as P

HIGHEST = lax.Precision.HIGHEST
F32 = jnp.float32
BF16 = jnp.bfloat16
LANES = 128


def halves(value):
    high = value.astype(BF16)
    return high, (value - high.astype(F32)).astype(BF16)


def table_halves(value):
    high = lax.reduce_precision(value, 8, 7)
    return high.astype(BF16), (value - high).astype(BF16)


def odd_frequencies(rows):
    angles = np.pi * np.outer(2 * np.arange(rows) + 1, np.arange(rows)) / (2 * rows)
    return np.cos(angles), -np.sin(angles)


def tables(rows, rates, freqs):
    cos_part, sin_part = odd_frequencies(rows)
    forward = jnp.asarray(np.concatenate([cos_part, sin_part], 0), F32)
    inverse = jnp.asarray(np.concatenate([cos_part, sin_part], 0).T / rows, F32)
    lags = jnp.arange(rows + 1).astype(F32)[None, :]
    decay = jnp.exp(-lags * rates[:, None])
    power_real = decay * jnp.cos(lags * freqs[:, None])
    power_imag = decay * jnp.sin(lags * freqs[:, None])
    to_start = jnp.concatenate([power_real[:, :rows], power_imag[:, :rows]], 0)
    to_end = jnp.concatenate([power_real[:, :0:-1], power_imag[:, :0:-1]], 0)
    left_g = jnp.concatenate(table_halves(jnp.concatenate([forward, to_start], 0)), 1)
    left_x = jnp.concatenate(table_halves(jnp.concatenate([forward, to_end], 0)), 1)
    back = jnp.concatenate(
        [inverse, power_real[:, :0:-1].T, -power_imag[:, :0:-1].T], 1
    )
    back_high, back_low = table_halves(back)
    basis_spectrum = jnp.dot(
        forward, power_real[:, :rows].T, precision=HIGHEST, preferred_element_type=F32
    )
    step = jnp.stack([power_real[:, rows], power_imag[:, rows]], 0)[:, :, None]
    return left_g, left_x, back_high, back_low, basis_spectrum, step


def side_by_side(ref, source, part):
    rows = ref.shape[2] // 2
    at = slice(part * rows, (part + 1) * rows)
    return jnp.concatenate([ref[source, 0, at, :], ref[source, 1, at, :]], 1)


def twice(value):
    return jnp.concatenate([value, value], 0)


def input_kernel(
    spans_ref,
    place_ref,
    g_ref,
    weight_ref,
    gain_ref,
    left_g_ref,
    back_high_ref,
    back_low_ref,
    spectrum_ref,
    step_ref,
    y_ref,
    states_ref,
    slot_of,
    sums,
    states,
    high,
    low,
):
    n_src, _, rows_dev, width = g_ref.shape
    rows = rows_dev // 2
    n_basis, lanes = weight_ref.shape
    n_spans = 2 * n_src
    n_own = n_src // 2
    own_base = place_ref[0] * n_own
    far_base = n_own - own_base
    for slot in range(n_spans):
        slot_of[spans_ref[slot]] = slot
    weight = weight_ref[...]
    taps = jnp.dot(spectrum_ref[...], weight, precision=HIGHEST, preferred_element_type=F32)
    taps_real, taps_imag = taps[:rows], taps[rows:]
    left = left_g_ref[...]
    for source in range(n_own):
        for part in range(2):
            far = twice(side_by_side(g_ref, far_base + source, part))
            sums[2 * (far_base + source) + part] = jnp.dot(
                left[2 * rows :], far, preferred_element_type=F32
            )
            near = twice(side_by_side(g_ref, own_base + source, part))
            of_g = jnp.dot(left, near, preferred_element_type=F32)
            sums[2 * (own_base + source) + part] = of_g[2 * rows :]
            g_real, g_imag = of_g[:rows], of_g[rows : 2 * rows]
            y_real = halves(taps_real * g_real + taps_imag * g_imag)
            y_imag = halves(taps_real * g_imag - taps_imag * g_real)
            slot = 2 * source + part
            high[slot, :rows] = y_real[0]
            high[slot, rows:] = y_imag[0]
            low[slot, :rows] = y_real[1]
            low[slot, rows:] = y_imag[1]
    step_real = jnp.broadcast_to(step_ref[0], (n_basis, lanes))
    step_imag = jnp.broadcast_to(step_ref[1], (n_basis, lanes))
    state_real = jnp.zeros((n_basis, lanes), F32)
    state_imag = jnp.zeros((n_basis, lanes), F32)
    for span in range(n_spans - 1, -1, -1):
        slot = slot_of[span]
        states[slot, :n_basis] = state_real
        states[slot, n_basis:] = state_imag
        if span:
            next_real = sums[slot, :n_basis] + step_real * state_real - step_imag * state_imag
            state_imag = sums[slot, n_basis:] + step_real * state_imag + step_imag * state_real
            state_real = next_real
    gain = gain_ref[...]
    back_high, back_low = back_high_ref[...], back_low_ref[...]
    both_weight = twice(weight)
    for source in range(n_own):
        for part in range(2):
            slot = 2 * source + part
            state = states[2 * own_base + slot]
            states_ref[slot] = state
            far = halves(both_weight * state)
            both_high = jnp.concatenate([high[slot], far[0]], 0)
            both_low = jnp.concatenate([low[slot], far[1]], 0)
            value = (
                jnp.dot(back_high, both_high, preferred_element_type=F32)
                + jnp.dot(back_high, both_low, preferred_element_type=F32)
                + jnp.dot(back_low, both_high, preferred_element_type=F32)
                + gain * side_by_side(g_ref, own_base + source, part).astype(F32)
            ).astype(BF16)
            at = slice(part * rows, (part + 1) * rows)
            y_ref[source, 0, at, :] = value[:, :width]
            y_ref[source, 1, at, :] = value[:, width:]


def weight_kernel(place_ref, g_ref, states_ref, left_g_ref, left_x_ref, spectrum_ref, *refs):
    x_refs, wgrad_ref = refs[:-1], refs[-1]
    n_own = len(x_refs)
    rows_dev, width = g_ref.shape[2:]
    rows = rows_dev // 2
    n_basis, lanes = states_ref.shape[1] // 2, states_ref.shape[2]
    half, own = place_ref[0], place_ref[1]
    left_g, left_x = left_g_ref[: 2 * rows], left_x_ref[...]
    cross_real = jnp.zeros((rows, lanes), F32)
    cross_imag = jnp.zeros((rows, lanes), F32)
    total = jnp.zeros((n_basis, lanes), F32)
    for offset, x_ref in enumerate(x_refs):
        source = own ^ offset
        for part in range(2):
            at = slice(part * rows, (part + 1) * rows)
            g = twice(side_by_side(g_ref, half * n_own + source, part))
            x = twice(jnp.concatenate([x_ref[0, at, :], x_ref[1, at, :]], 1))
            of_g = jnp.dot(left_g, g, preferred_element_type=F32)
            of_x = jnp.dot(left_x, x, preferred_element_type=F32)
            g_real, g_imag = of_g[:rows], of_g[rows:]
            x_real, x_imag = of_x[:rows], of_x[rows : 2 * rows]
            cross_real = cross_real + (x_real * g_real + x_imag * g_imag)
            cross_imag = cross_imag + (x_real * g_imag - x_imag * g_real)
            product = states_ref[2 * source + part] * of_x[2 * rows :]
            total = total + (product[:n_basis] - product[n_basis:])
    total = total + lax.dot_general(
        spectrum_ref[...],
        jnp.concatenate([cross_real, cross_imag], 0) * (1.0 / rows),
        (((0,), (0,)), ((), ())),
        precision=HIGHEST,
        preferred_element_type=F32,
    )
    for block in range(2):
        wgrad_ref[half ^ block] = total[:, block * width : (block + 1) * width]


def on_device(inputs, grad_out, filter_weight, filter_rates, filter_freqs, skip_gain, span_of_slot):
    rows_dev, channels = inputs.shape
    rows = rows_dev // 2
    n_basis = filter_weight.shape[0]
    devices = lax.axis_size("seq")
    position = lax.axis_index("seq")
    n_own = devices // 2
    half, rank = position // n_own, position % n_own
    own = channels // devices
    width = -(-own // LANES) * LANES
    lanes = 2 * width

    def widened(value):
        return jnp.pad(value, ((0, 0),) * (value.ndim - 1) + ((0, width - own),))

    def own_blocks(value):
        blocks = value.reshape(value.shape[0], 2, n_own, own)
        taken = lax.dynamic_index_in_dim(blocks, rank, 2, keepdims=False)
        return widened(taken).reshape(value.shape[0], lanes)

    blocks = grad_out.reshape(rows_dev, 2, n_own, own).transpose(2, 1, 0, 3)
    g = widened(lax.all_to_all(jnp.concatenate([blocks, blocks], 0), "seq", 0, 0, tiled=True))
    x_blocks = inputs.reshape(rows_dev, 2, n_own, own)
    x_parts = []
    for offset in range(n_own):
        part = lax.dynamic_index_in_dim(x_blocks, rank ^ offset, 2, keepdims=False)
        part = part.transpose(1, 0, 2)
        if offset:
            part = lax.ppermute(part, "seq", [(i, i ^ offset) for i in range(devices)])
        x_parts.append(widened(part))
    weight = own_blocks(filter_weight)
    gain = own_blocks(skip_gain[None, :])
    place = jnp.stack([half, rank]).astype(jnp.int32)
    left_g, left_x, back_high, back_low, spectrum, step = tables(
        rows, filter_rates, filter_freqs
    )
    n_spans = 2 * devices
    smem = pl.BlockSpec(memory_space=pltpu.SMEM)
    vmem = pl.BlockSpec(memory_space=pltpu.VMEM)
    params = pltpu.CompilerParams(vmem_limit_bytes=24 * 2**20)
    y, states = pl.pallas_call(
        input_kernel,
        out_shape=(
            jax.ShapeDtypeStruct((n_own, 2, rows_dev, width), BF16),
            jax.ShapeDtypeStruct((devices, 2 * n_basis, lanes), F32),
        ),
        in_specs=[smem, smem] + [vmem] * 8,
        out_specs=(vmem, vmem),
        scratch_shapes=[
            pltpu.SMEM((n_spans,), jnp.int32),
            pltpu.VMEM((n_spans, 2 * n_basis, lanes), F32),
            pltpu.VMEM((n_spans, 2 * n_basis, lanes), F32),
            pltpu.VMEM((devices, 2 * rows, lanes), BF16),
            pltpu.VMEM((devices, 2 * rows, lanes), BF16),
        ],
        compiler_params=params,
        name="input_part",
    )(span_of_slot, place, g, weight, gain, left_g, back_high, back_low, spectrum, step)
    y = lax.all_to_all(
        y[..., :own],
        "seq",
        0,
        0,
        tiled=True,
        axis_index_groups=[list(range(n_own)), list(range(n_own, devices))],
    )
    input_grad = y.transpose(2, 1, 0, 3).reshape(rows_dev, channels)
    wgrad = pl.pallas_call(
        weight_kernel,
        out_shape=jax.ShapeDtypeStruct((2, n_basis, width), F32),
        in_specs=[smem] + [vmem] * (5 + n_own),
        out_specs=vmem,
        compiler_params=params,
        cost_estimate=pl.CostEstimate(
            flops=8 * (rows + n_basis) * rows * n_spans * lanes,
            bytes_accessed=4 * n_spans * rows * lanes,
            transcendentals=0,
        ),
        name="weight_part",
    )(place, g, states, left_g, left_x, spectrum, *x_parts)
    other = lax.ppermute(wgrad[1], "seq", [(i, i ^ n_own) for i in range(devices)])
    return input_grad, (wgrad[0] + other)[:, :own]


def solution(mesh):
    placed = (
        P(("groups", "seq"), None),
        P(("groups", "seq"), None),
        P(),
        P(),
        P(),
        P(),
        P("groups"),
    )
    return jax.shard_map(
        on_device,
        mesh=mesh,
        in_specs=placed,
        out_specs=(P(("groups", "seq"), None), P("groups", "seq")),
        check_vma=False,
    )
```

```python
import functools
import math

import jax
import jax.numpy as jnp
import numpy as np
from jax import lax
from jax.experimental import pallas as pl
from jax.experimental.pallas import tpu as pltpu
from jax.sharding import PartitionSpec as P

HIGHEST = lax.Precision.HIGHEST
F32 = jnp.float32
BF16 = jnp.bfloat16
LANES = 128


def halves(value):
    high = value.astype(BF16)
    return high, (value - high.astype(F32)).astype(BF16)


def table_halves(value):
    high = lax.reduce_precision(value, 8, 7)
    return high.astype(BF16), (value - high).astype(BF16)


def odd_frequencies(rows):
    angles = np.pi * np.outer(2 * np.arange(rows) + 1, np.arange(rows)) / (2 * rows)
    return np.cos(angles), -np.sin(angles)


def tables(rows, rates, freqs):
    cos_part, sin_part = odd_frequencies(rows)
    forward = jnp.asarray(np.concatenate([cos_part, sin_part], 0), F32)
    inverse = jnp.asarray(np.concatenate([cos_part, sin_part], 0).T / rows, F32)
    lags = jnp.arange(rows + 1).astype(F32)[None, :]
    decay = jnp.exp(-lags * rates[:, None])
    power_real = decay * jnp.cos(lags * freqs[:, None])
    power_imag = decay * jnp.sin(lags * freqs[:, None])
    to_start = jnp.concatenate([power_real[:, :rows], power_imag[:, :rows]], 0)
    to_end = jnp.concatenate([power_real[:, :0:-1], power_imag[:, :0:-1]], 0)
    left_g = jnp.concatenate(table_halves(jnp.concatenate([forward, to_start], 0)), 1)
    left_x = jnp.concatenate(table_halves(jnp.concatenate([forward, to_end], 0)), 1)
    back = jnp.concatenate(
        [inverse, power_real[:, :0:-1].T, -power_imag[:, :0:-1].T], 1
    )
    back_high, back_low = table_halves(back)
    basis_spectrum = jnp.dot(
        forward, power_real[:, :rows].T, precision=HIGHEST, preferred_element_type=F32
    )
    step = jnp.stack([power_real[:, rows], power_imag[:, rows]], 0)[:, :, None]
    return left_g, left_x, back_high, back_low, basis_spectrum, step


def side_by_side(ref, source, part):
    rows = ref.shape[2] // 2
    at = slice(part * rows, (part + 1) * rows)
    return jnp.concatenate([ref[source, 0, at, :], ref[source, 1, at, :]], 1)


def twice(value):
    return jnp.concatenate([value, value], 0)


def input_kernel(
    spans_ref,
    place_ref,
    g_ref,
    weight_ref,
    gain_ref,
    left_g_ref,
    back_high_ref,
    back_low_ref,
    spectrum_ref,
    step_ref,
    y_ref,
    states_ref,
    slot_of,
    sums,
    states,
    high,
    low,
):
    n_src, _, rows_dev, width = g_ref.shape
    rows = rows_dev // 2
    n_basis, lanes = weight_ref.shape
    n_spans = 2 * n_src
    n_own = n_src // 2
    own_base = place_ref[0] * n_own
    far_base = n_own - own_base
    for slot in range(n_spans):
        slot_of[spans_ref[slot]] = slot
    weight = weight_ref[...]
    taps = jnp.dot(spectrum_ref[...], weight, precision=HIGHEST, preferred_element_type=F32)
    taps_real, taps_imag = taps[:rows], taps[rows:]
    left = left_g_ref[...]
    for source in range(n_own):
        for part in range(2):
            far = twice(side_by_side(g_ref, far_base + source, part))
            sums[2 * (far_base + source) + part] = jnp.dot(
                left[2 * rows :], far, preferred_element_type=F32
            )
            near = twice(side_by_side(g_ref, own_base + source, part))
            of_g = jnp.dot(left, near, preferred_element_type=F32)
            sums[2 * (own_base + source) + part] = of_g[2 * rows :]
            g_real, g_imag = of_g[:rows], of_g[rows : 2 * rows]
            y_real = halves(taps_real * g_real + taps_imag * g_imag)
            y_imag = halves(taps_real * g_imag - taps_imag * g_real)
            slot = 2 * source + part
            high[slot, :rows] = y_real[0]
            high[slot, rows:] = y_imag[0]
            low[slot, :rows] = y_real[1]
            low[slot, rows:] = y_imag[1]
    step_real = jnp.broadcast_to(step_ref[0], (n_basis, lanes))
    step_imag = jnp.broadcast_to(step_ref[1], (n_basis, lanes))
    state_real = jnp.zeros((n_basis, lanes), F32)
    state_imag = jnp.zeros((n_basis, lanes), F32)
    for span in range(n_spans - 1, -1, -1):
        slot = slot_of[span]
        states[slot, :n_basis] = state_real
        states[slot, n_basis:] = state_imag
        if span:
            next_real = sums[slot, :n_basis] + step_real * state_real - step_imag * state_imag
            state_imag = sums[slot, n_basis:] + step_real * state_imag + step_imag * state_real
            state_real = next_real
    gain = gain_ref[...]
    back_high, back_low = back_high_ref[...], back_low_ref[...]
    both_weight = twice(weight)
    for source in range(n_own):
        for part in range(2):
            slot = 2 * source + part
            state = states[2 * own_base + slot]
            states_ref[slot] = state
            far = halves(both_weight * state)
            both_high = jnp.concatenate([high[slot], far[0]], 0)
            both_low = jnp.concatenate([low[slot], far[1]], 0)
            value = (
                jnp.dot(back_high, both_high, preferred_element_type=F32)
                + jnp.dot(back_high, both_low, preferred_element_type=F32)
                + jnp.dot(back_low, both_high, preferred_element_type=F32)
                + gain * side_by_side(g_ref, own_base + source, part).astype(F32)
            ).astype(BF16)
            at = slice(part * rows, (part + 1) * rows)
            y_ref[source, 0, at, :] = value[:, :width]
            y_ref[source, 1, at, :] = value[:, width:]


def weight_kernel(place_ref, g_ref, states_ref, left_g_ref, left_x_ref, spectrum_ref, *refs):
    x_refs, wgrad_ref = refs[:-1], refs[-1]
    n_own = len(x_refs)
    rows_dev, width = g_ref.shape[2:]
    rows = rows_dev // 2
    n_basis, lanes = states_ref.shape[1] // 2, states_ref.shape[2]
    half, own = place_ref[0], place_ref[1]
    left_g, left_x = left_g_ref[: 2 * rows], left_x_ref[...]
    cross_real = jnp.zeros((rows, lanes), F32)
    cross_imag = jnp.zeros((rows, lanes), F32)
    total = jnp.zeros((n_basis, lanes), F32)
    for offset, x_ref in enumerate(x_refs):
        source = own ^ offset
        for part in range(2):
            at = slice(part * rows, (part + 1) * rows)
            g = twice(side_by_side(g_ref, half * n_own + source, part))
            x = twice(jnp.concatenate([x_ref[0, at, :], x_ref[1, at, :]], 1))
            of_g = jnp.dot(left_g, g, preferred_element_type=F32)
            of_x = jnp.dot(left_x, x, preferred_element_type=F32)
            g_real, g_imag = of_g[:rows], of_g[rows:]
            x_real, x_imag = of_x[:rows], of_x[rows : 2 * rows]
            cross_real = cross_real + (x_real * g_real + x_imag * g_imag)
            cross_imag = cross_imag + (x_real * g_imag - x_imag * g_real)
            product = states_ref[2 * source + part] * of_x[2 * rows :]
            total = total + (product[:n_basis] - product[n_basis:])
    total = total + lax.dot_general(
        spectrum_ref[...],
        jnp.concatenate([cross_real, cross_imag], 0) * (1.0 / rows),
        (((0,), (0,)), ((), ())),
        precision=HIGHEST,
        preferred_element_type=F32,
    )
    for block in range(2):
        wgrad_ref[half ^ block] = total[:, block * width : (block + 1) * width]


def on_device(inputs, grad_out, filter_weight, filter_rates, filter_freqs, skip_gain, span_of_slot):
    rows_dev, channels = inputs.shape
    rows = rows_dev // 2
    n_basis = filter_weight.shape[0]
    devices = lax.axis_size("seq")
    position = lax.axis_index("seq")
    n_own = devices // 2
    half, rank = position // n_own, position % n_own
    own = channels // devices
    width = -(-own // LANES) * LANES
    lanes = 2 * width

    def widened(value):
        return jnp.pad(value, ((0, 0),) * (value.ndim - 1) + ((0, width - own),))

    def own_blocks(value):
        blocks = value.reshape(value.shape[0], 2, n_own, own)
        taken = lax.dynamic_index_in_dim(blocks, rank, 2, keepdims=False)
        return widened(taken).reshape(value.shape[0], lanes)

    blocks = grad_out.reshape(rows_dev, 2, n_own, own).transpose(2, 1, 0, 3)
    g = widened(lax.all_to_all(jnp.concatenate([blocks, blocks], 0), "seq", 0, 0, tiled=True))
    left_g, left_x, back_high, back_low, spectrum, step = tables(
        rows, filter_rates, filter_freqs
    )
    later_inputs, spectrum = lax.optimization_barrier((inputs, spectrum))
    x_blocks = later_inputs.reshape(rows_dev, 2, n_own, own)
    x_parts = []
    for offset in range(n_own):
        part = lax.dynamic_index_in_dim(x_blocks, rank ^ offset, 2, keepdims=False)
        part = part.transpose(1, 0, 2)
        if offset:
            part = lax.ppermute(part, "seq", [(i, i ^ offset) for i in range(devices)])
        x_parts.append(widened(part))
    g, *x_parts = lax.optimization_barrier((g, *x_parts))
    weight = own_blocks(filter_weight)
    gain = own_blocks(skip_gain[None, :])
    place = jnp.stack([half, rank]).astype(jnp.int32)
    n_spans = 2 * devices
    smem = pl.BlockSpec(memory_space=pltpu.SMEM)
    vmem = pl.BlockSpec(memory_space=pltpu.VMEM)
    params = pltpu.CompilerParams(vmem_limit_bytes=24 * 2**20)
    y, states = pl.pallas_call(
        input_kernel,
        out_shape=(
            jax.ShapeDtypeStruct((n_own, 2, rows_dev, width), BF16),
            jax.ShapeDtypeStruct((devices, 2 * n_basis, lanes), F32),
        ),
        in_specs=[smem, smem] + [vmem] * 8,
        out_specs=(vmem, vmem),
        scratch_shapes=[
            pltpu.SMEM((n_spans,), jnp.int32),
            pltpu.VMEM((n_spans, 2 * n_basis, lanes), F32),
            pltpu.VMEM((n_spans, 2 * n_basis, lanes), F32),
            pltpu.VMEM((devices, 2 * rows, lanes), BF16),
            pltpu.VMEM((devices, 2 * rows, lanes), BF16),
        ],
        compiler_params=params,
        name="input_part",
    )(span_of_slot, place, g, weight, gain, left_g, back_high, back_low, spectrum, step)
    y = lax.all_to_all(
        y[..., :own],
        "seq",
        0,
        0,
        tiled=True,
        axis_index_groups=[list(range(n_own)), list(range(n_own, devices))],
    )
    input_grad = y.transpose(2, 1, 0, 3).reshape(rows_dev, channels)
    wgrad = pl.pallas_call(
        weight_kernel,
        out_shape=jax.ShapeDtypeStruct((2, n_basis, width), F32),
        in_specs=[smem] + [vmem] * (5 + n_own),
        out_specs=vmem,
        compiler_params=params,
        cost_estimate=pl.CostEstimate(
            flops=8 * (rows + n_basis) * rows * n_spans * lanes,
            bytes_accessed=4 * n_spans * rows * lanes,
            transcendentals=0,
        ),
        name="weight_part",
    )(place, g, states, left_g, left_x, spectrum, *x_parts)
    other = lax.ppermute(wgrad[1], "seq", [(i, i ^ n_own) for i in range(devices)])
    return input_grad, (wgrad[0] + other)[:, :own]


def solution(mesh):
    placed = (
        P(("groups", "seq"), None),
        P(("groups", "seq"), None),
        P(),
        P(),
        P(),
        P(),
        P("groups"),
    )
    return jax.shard_map(
        on_device,
        mesh=mesh,
        in_specs=placed,
        out_specs=(P(("groups", "seq"), None), P("groups", "seq")),
        check_vma=False,
    )
```

```python
import functools
import math

import jax
import jax.numpy as jnp
import numpy as np
from jax import lax
from jax.experimental import pallas as pl
from jax.experimental.pallas import tpu as pltpu
from jax.sharding import PartitionSpec as P

HIGHEST = lax.Precision.HIGHEST
F32 = jnp.float32
BF16 = jnp.bfloat16
LANES = 128


def halves(value):
    high = value.astype(BF16)
    return high, (value - high.astype(F32)).astype(BF16)


def table_halves(value):
    high = lax.reduce_precision(value, 8, 7)
    return high.astype(BF16), (value - high).astype(BF16)


def odd_frequencies(rows):
    angles = np.pi * np.outer(2 * np.arange(rows) + 1, np.arange(rows)) / (2 * rows)
    return np.cos(angles), -np.sin(angles)


def tables(rows, rates, freqs):
    cos_part, sin_part = odd_frequencies(rows)
    forward = jnp.asarray(np.concatenate([cos_part, sin_part], 0), F32)
    inverse = jnp.asarray(np.concatenate([cos_part, sin_part], 0).T / rows, F32)
    lags = jnp.arange(rows + 1).astype(F32)[None, :]
    decay = jnp.exp(-lags * rates[:, None])
    power_real = decay * jnp.cos(lags * freqs[:, None])
    power_imag = decay * jnp.sin(lags * freqs[:, None])
    to_start = jnp.concatenate([power_real[:, :rows], power_imag[:, :rows]], 0)
    to_end = jnp.concatenate([power_real[:, :0:-1], power_imag[:, :0:-1]], 0)
    left_g = jnp.concatenate(table_halves(jnp.concatenate([forward, to_start], 0)), 1)
    left_x = jnp.concatenate(table_halves(jnp.concatenate([forward, to_end], 0)), 1)
    back = jnp.concatenate(
        [inverse, power_real[:, :0:-1].T, -power_imag[:, :0:-1].T], 1
    )
    back_high, back_low = table_halves(back)
    basis_spectrum = jnp.dot(
        forward, power_real[:, :rows].T, precision=HIGHEST, preferred_element_type=F32
    )
    step = jnp.stack([power_real[:, rows], power_imag[:, rows]], 0)[:, :, None]
    return left_g, left_x, back_high, back_low, basis_spectrum, step


def side_by_side(ref, source, part):
    rows = ref.shape[2] // 2
    at = slice(part * rows, (part + 1) * rows)
    return jnp.concatenate([ref[source, 0, at, :], ref[source, 1, at, :]], 1)


def twice(value):
    return jnp.concatenate([value, value], 0)


def input_kernel(
    place_ref,
    g_ref,
    weight_ref,
    gain_ref,
    left_g_ref,
    back_high_ref,
    back_low_ref,
    spectrum_ref,
    step_ref,
    y_ref,
    states_ref,
    slot_of,
    sums,
    states,
    high,
    low,
):
    n_src, _, rows_dev, width = g_ref.shape
    rows = rows_dev // 2
    n_basis, lanes = weight_ref.shape
    n_spans = 2 * n_src
    n_own = n_src // 2
    own_base = place_ref[0] * n_own
    far_base = n_own - own_base
    for slot in range(n_spans):
        slot_of[place_ref[2 + slot]] = slot
    weight = weight_ref[...]
    taps = jnp.dot(spectrum_ref[...], weight, precision=HIGHEST, preferred_element_type=F32)
    taps_real, taps_imag = taps[:rows], taps[rows:]
    left = left_g_ref[...]
    for source in range(n_own):
        for part in range(2):
            far = twice(side_by_side(g_ref, far_base + source, part))
            sums[2 * (far_base + source) + part] = jnp.dot(
                left[2 * rows :], far, preferred_element_type=F32
            )
            near = twice(side_by_side(g_ref, own_base + source, part))
            of_g = jnp.dot(left, near, preferred_element_type=F32)
            sums[2 * (own_base + source) + part] = of_g[2 * rows :]
            g_real, g_imag = of_g[:rows], of_g[rows : 2 * rows]
            y_real = halves(taps_real * g_real + taps_imag * g_imag)
            y_imag = halves(taps_real * g_imag - taps_imag * g_real)
            slot = 2 * source + part
            high[slot, :rows] = y_real[0]
            high[slot, rows:] = y_imag[0]
            low[slot, :rows] = y_real[1]
            low[slot, rows:] = y_imag[1]
    step_real = jnp.broadcast_to(step_ref[0], (n_basis, lanes))
    step_imag = jnp.broadcast_to(step_ref[1], (n_basis, lanes))
    state_real = jnp.zeros((n_basis, lanes), F32)
    state_imag = jnp.zeros((n_basis, lanes), F32)
    for span in range(n_spans - 1, -1, -1):
        slot = slot_of[span]
        states[slot, :n_basis] = state_real
        states[slot, n_basis:] = state_imag
        if span:
            next_real = sums[slot, :n_basis] + step_real * state_real - step_imag * state_imag
            state_imag = sums[slot, n_basis:] + step_real * state_imag + step_imag * state_real
            state_real = next_real
    gain = gain_ref[...]
    back_high, back_low = back_high_ref[...], back_low_ref[...]
    both_weight = twice(weight)
    for source in range(n_own):
        for part in range(2):
            slot = 2 * source + part
            state = states[2 * own_base + slot]
            states_ref[slot] = state
            far = halves(both_weight * state)
            both_high = jnp.concatenate([high[slot], far[0]], 0)
            both_low = jnp.concatenate([low[slot], far[1]], 0)
            value = (
                jnp.dot(back_high, both_high, preferred_element_type=F32)
                + jnp.dot(back_high, both_low, preferred_element_type=F32)
                + jnp.dot(back_low, both_high, preferred_element_type=F32)
                + gain * side_by_side(g_ref, own_base + source, part).astype(F32)
            ).astype(BF16)
            at = slice(part * rows, (part + 1) * rows)
            y_ref[source, 0, at, :] = value[:, :width]
            y_ref[source, 1, at, :] = value[:, width:]


def weight_kernel(place_ref, g_ref, states_ref, left_g_ref, left_x_ref, spectrum_ref, *refs):
    x_refs, wgrad_ref = refs[:-1], refs[-1]
    n_own = len(x_refs)
    rows_dev, width = g_ref.shape[2:]
    rows = rows_dev // 2
    n_basis, lanes = states_ref.shape[1] // 2, states_ref.shape[2]
    half, own = place_ref[0], place_ref[1]
    left_g, left_x = left_g_ref[: 2 * rows], left_x_ref[...]
    cross_real = jnp.zeros((rows, lanes), F32)
    cross_imag = jnp.zeros((rows, lanes), F32)
    total = jnp.zeros((n_basis, lanes), F32)
    for offset, x_ref in enumerate(x_refs):
        source = own ^ offset
        for part in range(2):
            at = slice(part * rows, (part + 1) * rows)
            g = twice(side_by_side(g_ref, half * n_own + source, part))
            x = twice(jnp.concatenate([x_ref[0, at, :], x_ref[1, at, :]], 1))
            of_g = jnp.dot(left_g, g, preferred_element_type=F32)
            of_x = jnp.dot(left_x, x, preferred_element_type=F32)
            g_real, g_imag = of_g[:rows], of_g[rows:]
            x_real, x_imag = of_x[:rows], of_x[rows : 2 * rows]
            cross_real = cross_real + (x_real * g_real + x_imag * g_imag)
            cross_imag = cross_imag + (x_real * g_imag - x_imag * g_real)
            product = states_ref[2 * source + part] * of_x[2 * rows :]
            total = total + (product[:n_basis] - product[n_basis:])
    total = total + lax.dot_general(
        spectrum_ref[...],
        jnp.concatenate([cross_real, cross_imag], 0) * (1.0 / rows),
        (((0,), (0,)), ((), ())),
        precision=HIGHEST,
        preferred_element_type=F32,
    )
    for block in range(2):
        wgrad_ref[half ^ block] = total[:, block * width : (block + 1) * width]


def split_kernel(value_ref, parts_ref, sems):
    copies, groups, _, own = parts_ref.shape
    n_own = value_ref.shape[1] // (groups * own)
    moves = []
    for target in range(copies):
        for group in range(groups):
            at = (group * n_own + target % n_own) * own
            moves.append(
                pltpu.make_async_copy(
                    value_ref.at[:, at : at + own], parts_ref.at[target, group], sems.at[target, group]
                )
            )
    for move in moves:
        move.start()
    for move in moves:
        move.wait()


def join_kernel(parts_ref, value_ref, sems):
    n_own, groups, _, own = parts_ref.shape
    moves = []
    for source in range(n_own):
        for group in range(groups):
            at = (group * n_own + source) * own
            moves.append(
                pltpu.make_async_copy(
                    parts_ref.at[source, group], value_ref.at[:, at : at + own], sems.at[source, group]
                )
            )
    for move in moves:
        move.start()
    for move in moves:
        move.wait()


def on_device(inputs, grad_out, filter_weight, filter_rates, filter_freqs, skip_gain, span_of_slot):
    rows_dev, channels = inputs.shape
    rows = rows_dev // 2
    n_basis = filter_weight.shape[0]
    devices = lax.axis_size("seq")
    position = lax.axis_index("seq")
    n_own = devices // 2
    half, rank = position // n_own, position % n_own
    own = channels // devices
    width = -(-own // LANES) * LANES
    lanes = 2 * width

    def widened(value):
        return jnp.pad(value, ((0, 0),) * (value.ndim - 1) + ((0, width - own),))

    def own_blocks(value):
        blocks = value.reshape(value.shape[0], 2, n_own, own)
        taken = lax.dynamic_index_in_dim(blocks, rank, 2, keepdims=False)
        return widened(taken).reshape(value.shape[0], lanes)

    anywhere = pl.BlockSpec(memory_space=pl.ANY)
    small = pltpu.CompilerParams(vmem_limit_bytes=2**20)
    if own % LANES == 0:
        blocks = pl.pallas_call(
            split_kernel,
            out_shape=jax.ShapeDtypeStruct((devices, 2, rows_dev, own), BF16),
            in_specs=[anywhere],
            out_specs=anywhere,
            scratch_shapes=[pltpu.SemaphoreType.DMA((devices, 2))],
            compiler_params=small,
            name="split",
        )(grad_out)
    else:
        blocks = grad_out.reshape(rows_dev, 2, n_own, own).transpose(2, 1, 0, 3)
        blocks = jnp.concatenate([blocks, blocks], 0)
    g = widened(lax.all_to_all(blocks, "seq", 0, 0, tiled=True))
    left_g, left_x, back_high, back_low, spectrum, step = tables(
        rows, filter_rates, filter_freqs
    )
    later_inputs, spectrum = lax.optimization_barrier((inputs, spectrum))
    x_blocks = later_inputs.reshape(rows_dev, 2, n_own, own)
    x_parts = [None] * n_own
    for offset in range(n_own - 1, -1, -1):
        part = lax.dynamic_index_in_dim(x_blocks, rank ^ offset, 2, keepdims=False)
        part = part.transpose(1, 0, 2)
        if offset:
            part = lax.ppermute(part, "seq", [(i, i ^ offset) for i in range(devices)])
        x_parts[offset] = widened(part)
    weight = own_blocks(filter_weight)
    gain = own_blocks(skip_gain[None, :])
    g, *x_parts = lax.optimization_barrier((g, *x_parts))
    place = jnp.concatenate([jnp.stack([half, rank]).astype(jnp.int32), span_of_slot])
    n_spans = 2 * devices
    smem = pl.BlockSpec(memory_space=pltpu.SMEM)
    vmem = pl.BlockSpec(memory_space=pltpu.VMEM)
    params = pltpu.CompilerParams(vmem_limit_bytes=24 * 2**20)
    y, states = pl.pallas_call(
        input_kernel,
        out_shape=(
            jax.ShapeDtypeStruct((n_own, 2, rows_dev, width), BF16),
            jax.ShapeDtypeStruct((devices, 2 * n_basis, lanes), F32),
        ),
        in_specs=[smem] + [vmem] * 8,
        out_specs=(vmem, vmem),
        scratch_shapes=[
            pltpu.SMEM((n_spans,), jnp.int32),
            pltpu.VMEM((n_spans, 2 * n_basis, lanes), F32),
            pltpu.VMEM((n_spans, 2 * n_basis, lanes), F32),
            pltpu.VMEM((devices, 2 * rows, lanes), BF16),
            pltpu.VMEM((devices, 2 * rows, lanes), BF16),
        ],
        compiler_params=params,
        name="input_part",
    )(place, g, weight, gain, left_g, back_high, back_low, spectrum, step)
    y = lax.all_to_all(
        y[..., :own],
        "seq",
        0,
        0,
        tiled=True,
        axis_index_groups=[list(range(n_own)), list(range(n_own, devices))],
    )
    if own % LANES == 0:
        input_grad = pl.pallas_call(
            join_kernel,
            out_shape=jax.ShapeDtypeStruct((rows_dev, channels), BF16),
            in_specs=[anywhere],
            out_specs=anywhere,
            scratch_shapes=[pltpu.SemaphoreType.DMA((n_own, 2))],
            compiler_params=small,
            name="join",
        )(y)
    else:
        input_grad = y.transpose(2, 1, 0, 3).reshape(rows_dev, channels)
    wgrad = pl.pallas_call(
        weight_kernel,
        out_shape=jax.ShapeDtypeStruct((2, n_basis, width), F32),
        in_specs=[smem] + [vmem] * (5 + n_own),
        out_specs=vmem,
        compiler_params=params,
        cost_estimate=pl.CostEstimate(
            flops=8 * (rows + n_basis) * rows * n_spans * lanes,
            bytes_accessed=4 * n_spans * rows * lanes,
            transcendentals=0,
        ),
        name="weight_part",
    )(place, g, states, left_g, left_x, spectrum, *x_parts)
    other = lax.ppermute(wgrad[1], "seq", [(i, i ^ n_own) for i in range(devices)])
    return input_grad, (wgrad[0] + other)[:, :own]


def solution(mesh):
    placed = (
        P(("groups", "seq"), None),
        P(("groups", "seq"), None),
        P(),
        P(),
        P(),
        P(),
        P("groups"),
    )
    return jax.shard_map(
        on_device,
        mesh=mesh,
        in_specs=placed,
        out_specs=(P(("groups", "seq"), None), P("groups", "seq")),
        check_vma=False,
    )
```

```python
import functools
import math

import jax
import jax.numpy as jnp
import numpy as np
from jax import lax
from jax.experimental import pallas as pl
from jax.experimental.pallas import tpu as pltpu
from jax.sharding import PartitionSpec as P

HIGHEST = lax.Precision.HIGHEST
F32 = jnp.float32
BF16 = jnp.bfloat16
LANES = 128


def halves(value):
    high = value.astype(BF16)
    return high, (value - high.astype(F32)).astype(BF16)


def table_halves(value):
    high = lax.reduce_precision(value, 8, 7)
    return high.astype(BF16), (value - high).astype(BF16)


def odd_frequencies(rows):
    angles = np.pi * np.outer(2 * np.arange(rows) + 1, np.arange(rows)) / (2 * rows)
    return np.cos(angles), -np.sin(angles)


def tables(rows, rates, freqs, inputs):
    cos_part, sin_part = odd_frequencies(rows)
    forward = jnp.asarray(np.concatenate([cos_part, sin_part], 0), F32)
    inverse = jnp.asarray(np.concatenate([cos_part, sin_part], 0).T / rows, F32)
    lags = jnp.arange(rows + 1).astype(F32)[None, :]
    decay = jnp.exp(-lags * rates[:, None])
    power_real = decay * jnp.cos(lags * freqs[:, None])
    power_imag = decay * jnp.sin(lags * freqs[:, None])
    to_start = jnp.concatenate([power_real[:, :rows], power_imag[:, :rows]], 0)
    to_end = jnp.concatenate([power_real[:, :0:-1], power_imag[:, :0:-1]], 0)
    left_g = jnp.concatenate(table_halves(jnp.concatenate([forward, to_start], 0)), 1)
    left_x = jnp.concatenate(table_halves(jnp.concatenate([forward, to_end], 0)), 1)
    back = jnp.concatenate(
        [inverse, power_real[:, :0:-1].T, -power_imag[:, :0:-1].T], 1
    )
    back = jnp.concatenate(table_halves(back), 0)
    basis_spectrum = jnp.dot(
        forward, power_real[:, :rows].T, precision=HIGHEST, preferred_element_type=F32
    )
    later_inputs, basis_spectrum = lax.optimization_barrier((inputs, basis_spectrum))
    step = jnp.stack([power_real[:, rows], power_imag[:, rows]], 0)[:, :, None]
    return (left_g, left_x, back, basis_spectrum, step), later_inputs


def side_by_side(ref, source, part):
    rows = ref.shape[2] // 2
    at = slice(part * rows, (part + 1) * rows)
    return jnp.concatenate([ref[source, 0, at, :], ref[source, 1, at, :]], 1)


def twice(value):
    return jnp.concatenate([value, value], 0)


def input_kernel(
    place_ref,
    g_ref,
    weight_ref,
    gain_ref,
    left_g_ref,
    back_ref,
    spectrum_ref,
    step_ref,
    y_ref,
    states_ref,
    slot_of,
    sums,
    states,
    high,
    low,
):
    n_src, _, rows_dev, width = g_ref.shape
    rows = rows_dev // 2
    n_basis, lanes = weight_ref.shape
    n_spans = 2 * n_src
    n_own = n_src // 2
    own_base = place_ref[0] * n_own
    far_base = n_own - own_base
    for slot in range(n_spans):
        slot_of[place_ref[2 + slot]] = slot
    weight = weight_ref[...]
    taps = jnp.dot(spectrum_ref[...], weight, precision=HIGHEST, preferred_element_type=F32)
    taps_real, taps_imag = taps[:rows], taps[rows:]
    left = left_g_ref[...]
    for source in range(n_own):
        for part in range(2):
            far = twice(side_by_side(g_ref, far_base + source, part))
            sums[2 * (far_base + source) + part] = jnp.dot(
                left[2 * rows :], far, preferred_element_type=F32
            )
            near = twice(side_by_side(g_ref, own_base + source, part))
            of_g = jnp.dot(left, near, preferred_element_type=F32)
            sums[2 * (own_base + source) + part] = of_g[2 * rows :]
            g_real, g_imag = of_g[:rows], of_g[rows : 2 * rows]
            y_real = halves(taps_real * g_real + taps_imag * g_imag)
            y_imag = halves(taps_real * g_imag - taps_imag * g_real)
            slot = 2 * source + part
            high[slot, :rows] = y_real[0]
            high[slot, rows:] = y_imag[0]
            low[slot, :rows] = y_real[1]
            low[slot, rows:] = y_imag[1]
    step_real = jnp.broadcast_to(step_ref[0], (n_basis, lanes))
    step_imag = jnp.broadcast_to(step_ref[1], (n_basis, lanes))
    state_real = jnp.zeros((n_basis, lanes), F32)
    state_imag = jnp.zeros((n_basis, lanes), F32)
    for span in range(n_spans - 1, -1, -1):
        slot = slot_of[span]
        states[slot, :n_basis] = state_real
        states[slot, n_basis:] = state_imag
        if span:
            next_real = sums[slot, :n_basis] + step_real * state_real - step_imag * state_imag
            state_imag = sums[slot, n_basis:] + step_real * state_imag + step_imag * state_real
            state_real = next_real
    gain = gain_ref[...]
    both_weight = twice(weight)
    for source in range(n_own):
        for part in range(2):
            slot = 2 * source + part
            state = states[2 * own_base + slot]
            states_ref[slot] = state
            far = halves(both_weight * state)
            both_high = jnp.concatenate([high[slot], far[0]], 0)
            both_low = jnp.concatenate([low[slot], far[1]], 0)
            by_high = jnp.dot(back_ref[...], both_high, preferred_element_type=F32)
            value = (
                (by_high[:rows] + by_high[rows:])
                + jnp.dot(back_ref[:rows], both_low, preferred_element_type=F32)
                + gain * side_by_side(g_ref, own_base + source, part).astype(F32)
            ).astype(BF16)
            at = slice(part * rows, (part + 1) * rows)
            y_ref[source, 0, at, :] = value[:, :width]
            y_ref[source, 1, at, :] = value[:, width:]


def weight_kernel(place_ref, g_ref, states_ref, left_g_ref, left_x_ref, spectrum_ref, *refs):
    x_refs, wgrad_ref = refs[:-1], refs[-1]
    n_own = len(x_refs)
    rows_dev, width = g_ref.shape[2:]
    rows = rows_dev // 2
    n_basis, lanes = states_ref.shape[1] // 2, states_ref.shape[2]
    half, own = place_ref[0], place_ref[1]
    left_g, left_x = left_g_ref[: 2 * rows], left_x_ref[...]
    cross_real = jnp.zeros((rows, lanes), F32)
    cross_imag = jnp.zeros((rows, lanes), F32)
    total = jnp.zeros((n_basis, lanes), F32)
    for offset, x_ref in enumerate(x_refs):
        source = own ^ offset
        for part in range(2):
            at = slice(part * rows, (part + 1) * rows)
            g = twice(side_by_side(g_ref, half * n_own + source, part))
            x = twice(jnp.concatenate([x_ref[0, at, :], x_ref[1, at, :]], 1))
            of_g = jnp.dot(left_g, g, preferred_element_type=F32)
            of_x = jnp.dot(left_x, x, preferred_element_type=F32)
            g_real, g_imag = of_g[:rows], of_g[rows:]
            x_real, x_imag = of_x[:rows], of_x[rows : 2 * rows]
            cross_real = cross_real + (x_real * g_real + x_imag * g_imag)
            cross_imag = cross_imag + (x_real * g_imag - x_imag * g_real)
            product = states_ref[2 * source + part] * of_x[2 * rows :]
            total = total + (product[:n_basis] - product[n_basis:])
    total = total + lax.dot_general(
        spectrum_ref[...],
        jnp.concatenate([cross_real, cross_imag], 0) * (1.0 / rows),
        (((0,), (0,)), ((), ())),
        precision=HIGHEST,
        preferred_element_type=F32,
    )
    for block in range(2):
        wgrad_ref[half ^ block] = total[:, block * width : (block + 1) * width]


def split_kernel(value_ref, parts_ref, sems):
    copies, groups, _, own = parts_ref.shape
    n_own = value_ref.shape[1] // (groups * own)
    moves = []
    for target in range(copies):
        for group in range(groups):
            at = (group * n_own + target % n_own) * own
            moves.append(
                pltpu.make_async_copy(
                    value_ref.at[:, at : at + own], parts_ref.at[target, group], sems.at[target, group]
                )
            )
    for move in moves:
        move.start()
    for move in moves:
        move.wait()


def join_kernel(parts_ref, value_ref, sems):
    n_own, groups, _, own = parts_ref.shape
    moves = []
    for source in range(n_own):
        for group in range(groups):
            at = (group * n_own + source) * own
            moves.append(
                pltpu.make_async_copy(
                    parts_ref.at[source, group], value_ref.at[:, at : at + own], sems.at[source, group]
                )
            )
    for move in moves:
        move.start()
    for move in moves:
        move.wait()


def on_device(inputs, grad_out, filter_weight, filter_rates, filter_freqs, skip_gain, span_of_slot):
    rows_dev, channels = inputs.shape
    rows = rows_dev // 2
    n_basis = filter_weight.shape[0]
    devices = lax.axis_size("seq")
    position = lax.axis_index("seq")
    n_own = devices // 2
    half, rank = position // n_own, position % n_own
    own = channels // devices
    width = -(-own // LANES) * LANES
    lanes = 2 * width

    def widened(value):
        return jnp.pad(value, ((0, 0),) * (value.ndim - 1) + ((0, width - own),))

    def own_blocks(value):
        blocks = value.reshape(value.shape[0], 2, n_own, own)
        taken = lax.dynamic_index_in_dim(blocks, rank, 2, keepdims=False)
        return widened(taken).reshape(value.shape[0], lanes)

    anywhere = pl.BlockSpec(memory_space=pl.ANY)
    small = pltpu.CompilerParams(vmem_limit_bytes=2**20)
    if own % LANES == 0:
        blocks = pl.pallas_call(
            split_kernel,
            out_shape=jax.ShapeDtypeStruct((devices, 2, rows_dev, own), BF16),
            in_specs=[anywhere],
            out_specs=anywhere,
            scratch_shapes=[pltpu.SemaphoreType.DMA((devices, 2))],
            compiler_params=pltpu.CompilerParams(vmem_limit_bytes=60 * 2**20),
            name="split",
        )(grad_out)
    else:
        blocks = grad_out.reshape(rows_dev, 2, n_own, own).transpose(2, 1, 0, 3)
        blocks = jnp.concatenate([blocks, blocks], 0)
    g = widened(lax.all_to_all(blocks, "seq", 0, 0, tiled=True))
    made, later_inputs = tables(rows, filter_rates, filter_freqs, inputs)
    left_g, left_x, back, spectrum, step = made
    x_parts = [None] * n_own
    for offset in range(n_own - 1, -1, -1):
        taken = later_inputs if offset >= n_own // 2 else near_inputs
        x_blocks = taken.reshape(rows_dev, 2, n_own, own)
        part = lax.dynamic_index_in_dim(x_blocks, rank ^ offset, 2, keepdims=False)
        part = part.transpose(1, 0, 2)
        if offset:
            part = lax.ppermute(part, "seq", [(i, i ^ offset) for i in range(devices)])
        if offset == n_own - 1:
            near_inputs, part = lax.optimization_barrier((later_inputs, part))
        x_parts[offset] = widened(part)
    weight = own_blocks(filter_weight)
    gain = own_blocks(skip_gain[None, :])
    g, *x_parts = lax.optimization_barrier((g, *x_parts))
    place = jnp.concatenate([jnp.stack([half, rank]).astype(jnp.int32), span_of_slot])
    n_spans = 2 * devices
    smem = pl.BlockSpec(memory_space=pltpu.SMEM)
    vmem = pl.BlockSpec(memory_space=pltpu.VMEM)
    params = pltpu.CompilerParams(vmem_limit_bytes=24 * 2**20)
    y, states = pl.pallas_call(
        input_kernel,
        out_shape=(
            jax.ShapeDtypeStruct((n_own, 2, rows_dev, width), BF16),
            jax.ShapeDtypeStruct((devices, 2 * n_basis, lanes), F32),
        ),
        in_specs=[smem] + [vmem] * 7,
        out_specs=(vmem, vmem),
        scratch_shapes=[
            pltpu.SMEM((n_spans,), jnp.int32),
            pltpu.VMEM((n_spans, 2 * n_basis, lanes), F32),
            pltpu.VMEM((n_spans, 2 * n_basis, lanes), F32),
            pltpu.VMEM((devices, 2 * rows, lanes), BF16),
            pltpu.VMEM((devices, 2 * rows, lanes), BF16),
        ],
        compiler_params=params,
        name="input_part",
    )(place, g, weight, gain, left_g, back, spectrum, step)
    y = lax.all_to_all(
        y[..., :own],
        "seq",
        0,
        0,
        tiled=True,
        axis_index_groups=[list(range(n_own)), list(range(n_own, devices))],
    )
    if own % LANES == 0:
        input_grad = pl.pallas_call(
            join_kernel,
            out_shape=jax.ShapeDtypeStruct((rows_dev, channels), BF16),
            in_specs=[anywhere],
            out_specs=anywhere,
            scratch_shapes=[pltpu.SemaphoreType.DMA((n_own, 2))],
            compiler_params=small,
            name="join",
        )(y)
    else:
        input_grad = y.transpose(2, 1, 0, 3).reshape(rows_dev, channels)
    wgrad = pl.pallas_call(
        weight_kernel,
        out_shape=jax.ShapeDtypeStruct((2, n_basis, width), F32),
        in_specs=[smem] + [vmem] * (5 + n_own),
        out_specs=vmem,
        compiler_params=params,
        cost_estimate=pl.CostEstimate(
            flops=8 * (rows + n_basis) * rows * n_spans * lanes,
            bytes_accessed=4 * n_spans * rows * lanes,
            transcendentals=0,
        ),
        name="weight_part",
    )(place, g, states, left_g, left_x, spectrum, *x_parts)
    other = lax.ppermute(wgrad[1], "seq", [(i, i ^ n_own) for i in range(devices)])
    return input_grad, (wgrad[0] + other)[:, :own]


def solution(mesh):
    placed = (
        P(("groups", "seq"), None),
        P(("groups", "seq"), None),
        P(),
        P(),
        P(),
        P(),
        P("groups"),
    )
    return jax.shard_map(
        on_device,
        mesh=mesh,
        in_specs=placed,
        out_specs=(P(("groups", "seq"), None), P("groups", "seq")),
        check_vma=False,
    )
```

```python
import functools
import math

import jax
import jax.numpy as jnp
import numpy as np
from jax import lax
from jax.experimental import pallas as pl
from jax.experimental.pallas import tpu as pltpu
from jax.sharding import PartitionSpec as P

HIGHEST = lax.Precision.HIGHEST
F32 = jnp.float32
BF16 = jnp.bfloat16
LANES = 128


def halves(value):
    high = value.astype(BF16)
    return high, (value - high.astype(F32)).astype(BF16)


def table_halves(value):
    high = lax.reduce_precision(value, 8, 7)
    return high.astype(BF16), (value - high).astype(BF16)


def odd_frequencies(rows):
    angles = np.pi * np.outer(2 * np.arange(rows) + 1, np.arange(rows)) / (2 * rows)
    return np.cos(angles), -np.sin(angles)


def tables(rows, rates, freqs, inputs):
    cos_part, sin_part = odd_frequencies(rows)
    forward = jnp.asarray(np.concatenate([cos_part, sin_part], 0), F32)
    inverse = jnp.asarray(np.concatenate([cos_part, sin_part], 0).T / rows, F32)
    lags = jnp.arange(rows + 1).astype(F32)[None, :]
    decay = jnp.exp(-lags * rates[:, None])
    power_real = decay * jnp.cos(lags * freqs[:, None])
    power_imag = decay * jnp.sin(lags * freqs[:, None])
    to_start = jnp.concatenate([power_real[:, :rows], power_imag[:, :rows]], 0)
    to_end = jnp.concatenate([power_real[:, :0:-1], power_imag[:, :0:-1]], 0)
    left_g = jnp.concatenate(table_halves(jnp.concatenate([forward, to_start], 0)), 1)
    left_x = jnp.concatenate(table_halves(jnp.concatenate([forward, to_end], 0)), 1)
    back = jnp.concatenate(
        [inverse, power_real[:, :0:-1].T, -power_imag[:, :0:-1].T], 1
    )
    back = jnp.concatenate(table_halves(back), 0)
    basis_spectrum = jnp.dot(
        forward, power_real[:, :rows].T, precision=HIGHEST, preferred_element_type=F32
    )
    later_inputs, basis_spectrum = lax.optimization_barrier((inputs, basis_spectrum))
    step = jnp.stack([power_real[:, rows], power_imag[:, rows]], 0)[:, :, None]
    return (left_g, left_x, back, basis_spectrum, step), later_inputs


def side_by_side(ref, source, part):
    rows = ref.shape[2] // 2
    at = slice(part * rows, (part + 1) * rows)
    return jnp.concatenate([ref[source, 0, at, :], ref[source, 1, at, :]], 1)


def twice(value):
    return jnp.concatenate([value, value], 0)


def input_kernel(
    place_ref,
    g_ref,
    weight_ref,
    gain_ref,
    left_g_ref,
    back_ref,
    spectrum_ref,
    step_ref,
    y_ref,
    states_ref,
    slot_of,
    sums,
    states,
    high,
    low,
    result,
    sems,
):
    n_src, _, rows_dev, width = g_ref.shape
    rows = rows_dev // 2
    n_basis, lanes = weight_ref.shape
    n_spans = 2 * n_src
    n_own = n_src // 2
    own_base = place_ref[0] * n_own
    far_base = n_own - own_base
    for slot in range(n_spans):
        slot_of[place_ref[2 + slot]] = slot
    weight = weight_ref[...]
    taps = jnp.dot(spectrum_ref[...], weight, precision=HIGHEST, preferred_element_type=F32)
    taps_real, taps_imag = taps[:rows], taps[rows:]
    left = left_g_ref[...]
    for source in range(n_own):
        for part in range(2):
            far = twice(side_by_side(g_ref, far_base + source, part))
            sums[2 * (far_base + source) + part] = jnp.dot(
                left[2 * rows :], far, preferred_element_type=F32
            )
            near = twice(side_by_side(g_ref, own_base + source, part))
            of_g = jnp.dot(left, near, preferred_element_type=F32)
            sums[2 * (own_base + source) + part] = of_g[2 * rows :]
            g_real, g_imag = of_g[:rows], of_g[rows : 2 * rows]
            y_real = halves(taps_real * g_real + taps_imag * g_imag)
            y_imag = halves(taps_real * g_imag - taps_imag * g_real)
            slot = 2 * source + part
            high[slot, :rows] = y_real[0]
            high[slot, rows:] = y_imag[0]
            low[slot, :rows] = y_real[1]
            low[slot, rows:] = y_imag[1]
    step_real = jnp.broadcast_to(step_ref[0], (n_basis, lanes))
    step_imag = jnp.broadcast_to(step_ref[1], (n_basis, lanes))
    state_real = jnp.zeros((n_basis, lanes), F32)
    state_imag = jnp.zeros((n_basis, lanes), F32)
    for span in range(n_spans - 1, -1, -1):
        slot = slot_of[span]
        states[slot, :n_basis] = state_real
        states[slot, n_basis:] = state_imag
        if span:
            next_real = sums[slot, :n_basis] + step_real * state_real - step_imag * state_imag
            state_imag = sums[slot, n_basis:] + step_real * state_imag + step_imag * state_real
            state_real = next_real
    gain = gain_ref[...]
    both_weight = twice(weight)
    leaving = []
    for source in range(n_own):
        for part in range(2):
            slot = 2 * source + part
            state = states[2 * own_base + slot]
            states_ref[slot] = state
            far = halves(both_weight * state)
            both_high = jnp.concatenate([high[slot], far[0]], 0)
            both_low = jnp.concatenate([low[slot], far[1]], 0)
            by_high = jnp.dot(back_ref[...], both_high, preferred_element_type=F32)
            value = (
                (by_high[:rows] + by_high[rows:])
                + jnp.dot(back_ref[:rows], both_low, preferred_element_type=F32)
                + gain * side_by_side(g_ref, own_base + source, part).astype(F32)
            ).astype(BF16)
            at = slice(part * rows, (part + 1) * rows)
            result[source, 0, at, :] = value[:, :width]
            result[source, 1, at, :] = value[:, width:]
        leaving.append(
            pltpu.make_async_copy(result.at[source], y_ref.at[source], sems.at[source])
        )
        leaving[-1].start()
    for move in leaving:
        move.wait()


def weight_kernel(place_ref, g_ref, states_ref, left_g_ref, left_x_ref, spectrum_ref, *refs):
    x_refs, wgrad_ref = refs[:-1], refs[-1]
    n_own = len(x_refs)
    rows_dev, width = g_ref.shape[2:]
    rows = rows_dev // 2
    n_basis, lanes = states_ref.shape[1] // 2, states_ref.shape[2]
    half, own = place_ref[0], place_ref[1]
    left_g, left_x = left_g_ref[: 2 * rows], left_x_ref[...]
    cross_real = jnp.zeros((rows, lanes), F32)
    cross_imag = jnp.zeros((rows, lanes), F32)
    total = jnp.zeros((n_basis, lanes), F32)
    for offset, x_ref in enumerate(x_refs):
        source = own ^ offset
        for part in range(2):
            at = slice(part * rows, (part + 1) * rows)
            g = twice(side_by_side(g_ref, half * n_own + source, part))
            x = twice(jnp.concatenate([x_ref[0, at, :], x_ref[1, at, :]], 1))
            of_g = jnp.dot(left_g, g, preferred_element_type=F32)
            of_x = jnp.dot(left_x, x, preferred_element_type=F32)
            g_real, g_imag = of_g[:rows], of_g[rows:]
            x_real, x_imag = of_x[:rows], of_x[rows : 2 * rows]
            cross_real = cross_real + (x_real * g_real + x_imag * g_imag)
            cross_imag = cross_imag + (x_real * g_imag - x_imag * g_real)
            product = states_ref[2 * source + part] * of_x[2 * rows :]
            total = total + (product[:n_basis] - product[n_basis:])
    total = total + lax.dot_general(
        spectrum_ref[...],
        jnp.concatenate([cross_real, cross_imag], 0) * (1.0 / rows),
        (((0,), (0,)), ((), ())),
        precision=HIGHEST,
        preferred_element_type=F32,
    )
    for block in range(2):
        wgrad_ref[half ^ block] = total[:, block * width : (block + 1) * width]


def split_kernel(value_ref, parts_ref, held, parts, sems_in, sems_out):
    n_own, groups, rows_dev, own = parts.shape
    chunks = sems_in.shape[0]
    rows = rows_dev // chunks
    copies = parts_ref.shape[0] // n_own
    arrivals = []
    for chunk in range(chunks):
        at = pl.ds(chunk * rows, rows)
        arrivals.append(pltpu.make_async_copy(value_ref.at[at], held.at[at], sems_in.at[chunk]))
        arrivals[-1].start()
    leaving = []
    for chunk in range(chunks):
        at = pl.ds(chunk * rows, rows)
        arrivals[chunk].wait()
        for target in range(n_own):
            for group in range(groups):
                column = (group * n_own + target) * own
                parts[target, group, at] = held[at, column : column + own]
        for copy in range(copies):
            leaving.append(
                pltpu.make_async_copy(
                    parts.at[:, :, at],
                    parts_ref.at[pl.ds(copy * n_own, n_own), :, at],
                    sems_out.at[chunk, copy],
                )
            )
            leaving[-1].start()
    for move in leaving:
        move.wait()


def join_kernel(parts_ref, value_ref, sems):
    n_own, groups, _, own = parts_ref.shape
    moves = []
    for source in range(n_own):
        for group in range(groups):
            at = (group * n_own + source) * own
            moves.append(
                pltpu.make_async_copy(
                    parts_ref.at[source, group], value_ref.at[:, at : at + own], sems.at[source, group]
                )
            )
    for move in moves:
        move.start()
    for move in moves:
        move.wait()


def on_device(inputs, grad_out, filter_weight, filter_rates, filter_freqs, skip_gain, span_of_slot):
    rows_dev, channels = inputs.shape
    rows = rows_dev // 2
    n_basis = filter_weight.shape[0]
    devices = lax.axis_size("seq")
    position = lax.axis_index("seq")
    n_own = devices // 2
    half, rank = position // n_own, position % n_own
    own = channels // devices
    width = -(-own // LANES) * LANES
    lanes = 2 * width

    def widened(value):
        return jnp.pad(value, ((0, 0),) * (value.ndim - 1) + ((0, width - own),))

    def own_blocks(value):
        blocks = value.reshape(value.shape[0], 2, n_own, own)
        taken = lax.dynamic_index_in_dim(blocks, rank, 2, keepdims=False)
        return widened(taken).reshape(value.shape[0], lanes)

    anywhere = pl.BlockSpec(memory_space=pl.ANY)
    small = pltpu.CompilerParams(vmem_limit_bytes=2**20)
    if own % LANES == 0:
        blocks = pl.pallas_call(
            split_kernel,
            out_shape=jax.ShapeDtypeStruct((devices, 2, rows_dev, own), BF16),
            in_specs=[pl.BlockSpec(memory_space=pltpu.HBM)],
            out_specs=anywhere,
            scratch_shapes=[
                pltpu.VMEM((rows_dev, channels), BF16),
                pltpu.VMEM((n_own, 2, rows_dev, own), BF16),
                pltpu.SemaphoreType.DMA((4,)),
                pltpu.SemaphoreType.DMA((4, 2)),
            ],
            compiler_params=pltpu.CompilerParams(vmem_limit_bytes=60 * 2**20),
            name="split",
        )(grad_out)
    else:
        blocks = grad_out.reshape(rows_dev, 2, n_own, own).transpose(2, 1, 0, 3)
        blocks = jnp.concatenate([blocks, blocks], 0)
    g = widened(lax.all_to_all(blocks, "seq", 0, 0, tiled=True))
    made, later_inputs = tables(rows, filter_rates, filter_freqs, inputs)
    left_g, left_x, back, spectrum, step = made
    x_blocks = later_inputs.reshape(rows_dev, 2, n_own, own)
    x_parts = []
    for offset in range(n_own):
        part = lax.dynamic_index_in_dim(x_blocks, rank ^ offset, 2, keepdims=False)
        part = part.transpose(1, 0, 2)
        if offset:
            part = lax.ppermute(part, "seq", [(i, i ^ offset) for i in range(devices)])
        x_parts.append(widened(part))
    weight = own_blocks(filter_weight)
    gain = own_blocks(skip_gain[None, :])
    place = jnp.concatenate([jnp.stack([half, rank]).astype(jnp.int32), span_of_slot])
    n_spans = 2 * devices
    smem = pl.BlockSpec(memory_space=pltpu.SMEM)
    vmem = pl.BlockSpec(memory_space=pltpu.VMEM)
    params = pltpu.CompilerParams(vmem_limit_bytes=24 * 2**20)
    y, states = pl.pallas_call(
        input_kernel,
        out_shape=(
            jax.ShapeDtypeStruct((n_own, 2, rows_dev, width), BF16),
            jax.ShapeDtypeStruct((devices, 2 * n_basis, lanes), F32),
        ),
        in_specs=[smem] + [vmem] * 7,
        out_specs=(anywhere, vmem),
        scratch_shapes=[
            pltpu.SMEM((n_spans,), jnp.int32),
            pltpu.VMEM((n_spans, 2 * n_basis, lanes), F32),
            pltpu.VMEM((n_spans, 2 * n_basis, lanes), F32),
            pltpu.VMEM((devices, 2 * rows, lanes), BF16),
            pltpu.VMEM((devices, 2 * rows, lanes), BF16),
            pltpu.VMEM((n_own, 2, rows_dev, width), BF16),
            pltpu.SemaphoreType.DMA((n_own,)),
        ],
        compiler_params=params,
        cost_estimate=pl.CostEstimate(flops=4*10**10, bytes_accessed=2**20, transcendentals=0),
        name="input_part",
    )(place, g, weight, gain, left_g, back, spectrum, step)
    y = lax.all_to_all(
        y[..., :own],
        "seq",
        0,
        0,
        tiled=True,
        axis_index_groups=[list(range(n_own)), list(range(n_own, devices))],
    )
    if own % LANES == 0:
        input_grad = pl.pallas_call(
            join_kernel,
            out_shape=jax.ShapeDtypeStruct((rows_dev, channels), BF16),
            in_specs=[anywhere],
            out_specs=anywhere,
            scratch_shapes=[pltpu.SemaphoreType.DMA((n_own, 2))],
            compiler_params=small,
            name="join",
        )(y)
    else:
        input_grad = y.transpose(2, 1, 0, 3).reshape(rows_dev, channels)
    wgrad = pl.pallas_call(
        weight_kernel,
        out_shape=jax.ShapeDtypeStruct((2, n_basis, width), F32),
        in_specs=[smem] + [vmem] * (5 + n_own),
        out_specs=vmem,
        compiler_params=params,
        cost_estimate=pl.CostEstimate(
            flops=50 * 8 * (rows + n_basis) * rows * n_spans * lanes,
            bytes_accessed=4 * n_spans * rows * lanes,
            transcendentals=0,
        ),
        name="weight_part",
    )(place, g, states, left_g, left_x, spectrum, *x_parts)
    other = lax.ppermute(wgrad[1], "seq", [(i, i ^ n_own) for i in range(devices)])
    return input_grad, (wgrad[0] + other)[:, :own]


def solution(mesh):
    placed = (
        P(("groups", "seq"), None),
        P(("groups", "seq"), None),
        P(),
        P(),
        P(),
        P(),
        P("groups"),
    )
    return jax.shard_map(
        on_device,
        mesh=mesh,
        in_specs=placed,
        out_specs=(P(("groups", "seq"), None), P("groups", "seq")),
        check_vma=False,
    )
```

```python
import functools
import math

import jax
import jax.numpy as jnp
import numpy as np
from jax import lax
from jax.experimental import pallas as pl
from jax.experimental.pallas import tpu as pltpu
from jax.sharding import PartitionSpec as P

HIGHEST = lax.Precision.HIGHEST
F32 = jnp.float32
BF16 = jnp.bfloat16
LANES = 128


def halves(value):
    high = value.astype(BF16)
    return high, (value - high.astype(F32)).astype(BF16)


def table_halves(value):
    high = lax.reduce_precision(value, 8, 7)
    return high.astype(BF16), (value - high).astype(BF16)


def odd_frequencies(rows):
    angles = np.pi * np.outer(2 * np.arange(rows) + 1, np.arange(rows)) / (2 * rows)
    return np.cos(angles), -np.sin(angles)


def tables(rows, rates, freqs):
    cos_part, sin_part = odd_frequencies(rows)
    forward = jnp.asarray(np.concatenate([cos_part, sin_part], 0), F32)
    inverse = jnp.asarray(np.concatenate([cos_part, sin_part], 0).T / rows, F32)
    lags = jnp.arange(rows + 1).astype(F32)[None, :]
    decay = jnp.exp(-lags * rates[:, None])
    power_real = decay * jnp.cos(lags * freqs[:, None])
    power_imag = decay * jnp.sin(lags * freqs[:, None])
    to_start = jnp.concatenate([power_real[:, :rows], power_imag[:, :rows]], 0)
    to_end = jnp.concatenate([power_real[:, :0:-1], power_imag[:, :0:-1]], 0)
    left_g = jnp.concatenate(table_halves(jnp.concatenate([forward, to_start], 0)), 1)
    left_x = jnp.concatenate(table_halves(jnp.concatenate([forward, to_end], 0)), 1)
    back = jnp.concatenate(
        [inverse, power_real[:, :0:-1].T, -power_imag[:, :0:-1].T], 1
    )
    back = jnp.concatenate(table_halves(back), 0)
    basis_spectrum = jnp.dot(
        forward, power_real[:, :rows].T, precision=HIGHEST, preferred_element_type=F32
    )
    step = jnp.stack([power_real[:, rows], power_imag[:, rows]], 0)[:, :, None]
    return left_g, left_x, back, basis_spectrum, step


def side_by_side(ref, source, part):
    rows = ref.shape[2] // 2
    at = slice(part * rows, (part + 1) * rows)
    return jnp.concatenate([ref[source, 0, at, :], ref[source, 1, at, :]], 1)


def twice(value):
    return jnp.concatenate([value, value], 0)


def input_kernel(
    place_ref,
    g_ref,
    weight_ref,
    gain_ref,
    left_g_ref,
    back_ref,
    spectrum_ref,
    step_ref,
    y_ref,
    states_ref,
    slot_of,
    sums,
    states,
    high,
    low,
    result,
    sems,
):
    n_src, _, rows_dev, width = g_ref.shape
    rows = rows_dev // 2
    n_basis, lanes = weight_ref.shape
    n_spans = 2 * n_src
    n_own = n_src // 2
    own_base = place_ref[0] * n_own
    far_base = n_own - own_base
    for slot in range(n_spans):
        slot_of[place_ref[2 + slot]] = slot
    weight = weight_ref[...]
    taps = jnp.dot(spectrum_ref[...], weight, precision=HIGHEST, preferred_element_type=F32)
    taps_real, taps_imag = taps[:rows], taps[rows:]
    left = left_g_ref[...]
    for source in range(n_own):
        for part in range(2):
            far = twice(side_by_side(g_ref, far_base + source, part))
            sums[2 * (far_base + source) + part] = jnp.dot(
                left[2 * rows :], far, preferred_element_type=F32
            )
            near = twice(side_by_side(g_ref, own_base + source, part))
            of_g = jnp.dot(left, near, preferred_element_type=F32)
            sums[2 * (own_base + source) + part] = of_g[2 * rows :]
            g_real, g_imag = of_g[:rows], of_g[rows : 2 * rows]
            y_real = halves(taps_real * g_real + taps_imag * g_imag)
            y_imag = halves(taps_real * g_imag - taps_imag * g_real)
            slot = 2 * source + part
            high[slot, :rows] = y_real[0]
            high[slot, rows:] = y_imag[0]
            low[slot, :rows] = y_real[1]
            low[slot, rows:] = y_imag[1]
    step_real = jnp.broadcast_to(step_ref[0], (n_basis, lanes))
    step_imag = jnp.broadcast_to(step_ref[1], (n_basis, lanes))
    state_real = jnp.zeros((n_basis, lanes), F32)
    state_imag = jnp.zeros((n_basis, lanes), F32)
    for span in range(n_spans - 1, -1, -1):
        slot = slot_of[span]
        states[slot, :n_basis] = state_real
        states[slot, n_basis:] = state_imag
        if span:
            next_real = sums[slot, :n_basis] + step_real * state_real - step_imag * state_imag
            state_imag = sums[slot, n_basis:] + step_real * state_imag + step_imag * state_real
            state_real = next_real
    gain = gain_ref[...]
    both_weight = twice(weight)
    leaving = []
    for source in range(n_own):
        for part in range(2):
            slot = 2 * source + part
            state = states[2 * own_base + slot]
            states_ref[slot] = state
            far = halves(both_weight * state)
            both_high = jnp.concatenate([high[slot], far[0]], 0)
            both_low = jnp.concatenate([low[slot], far[1]], 0)
            by_high = jnp.dot(back_ref[...], both_high, preferred_element_type=F32)
            value = (
                (by_high[:rows] + by_high[rows:])
                + jnp.dot(back_ref[:rows], both_low, preferred_element_type=F32)
                + gain * side_by_side(g_ref, own_base + source, part).astype(F32)
            ).astype(BF16)
            at = slice(part * rows, (part + 1) * rows)
            result[source, 0, at, :] = value[:, :width]
            result[source, 1, at, :] = value[:, width:]
        leaving.append(
            pltpu.make_async_copy(result.at[source], y_ref.at[source], sems.at[source])
        )
        leaving[-1].start()
    for move in leaving:
        move.wait()


def weight_kernel(place_ref, g_ref, states_ref, left_g_ref, left_x_ref, spectrum_ref, x_ref, wgrad_ref):
    n_own = x_ref.shape[0]
    bits = n_own.bit_length() - 1
    rows_dev, width = g_ref.shape[2:]
    rows = rows_dev // 2
    n_basis, lanes = states_ref.shape[1] // 2, states_ref.shape[2]
    half, own = place_ref[0], place_ref[1]
    left_g, left_x = left_g_ref[: 2 * rows], left_x_ref[...]
    cross_real = jnp.zeros((rows, lanes), F32)
    cross_imag = jnp.zeros((rows, lanes), F32)
    total = jnp.zeros((n_basis, lanes), F32)
    for index in range(n_own):
        source = own ^ sum((index >> bit & 1) << (bits - 1 - bit) for bit in range(bits))
        for part in range(2):
            g = twice(side_by_side(g_ref, half * n_own + source, part))
            x = twice(side_by_side(x_ref, index, part))
            of_g = jnp.dot(left_g, g, preferred_element_type=F32)
            of_x = jnp.dot(left_x, x, preferred_element_type=F32)
            g_real, g_imag = of_g[:rows], of_g[rows:]
            x_real, x_imag = of_x[:rows], of_x[rows : 2 * rows]
            cross_real = cross_real + (x_real * g_real + x_imag * g_imag)
            cross_imag = cross_imag + (x_real * g_imag - x_imag * g_real)
            product = states_ref[2 * source + part] * of_x[2 * rows :]
            total = total + (product[:n_basis] - product[n_basis:])
    total = total + lax.dot_general(
        spectrum_ref[...],
        jnp.concatenate([cross_real, cross_imag], 0) * (1.0 / rows),
        (((0,), (0,)), ((), ())),
        precision=HIGHEST,
        preferred_element_type=F32,
    )
    for block in range(2):
        wgrad_ref[half ^ block] = total[:, block * width : (block + 1) * width]


def split_kernel(side_ref, g_ref, x_ref, g_parts_ref, x_parts_ref, g_held, x_held, g_parts, sems_in, sems_out):
    n_own, groups, rows_dev, own = g_parts.shape
    n_side = n_own // 2
    chunks = sems_in.shape[0]
    rows = rows_dev // chunks
    arrivals = []
    for chunk in range(chunks):
        at = pl.ds(chunk * rows, rows)
        for index, (whole_ref, held) in enumerate(((g_ref, g_held), (x_ref, x_held))):
            move = pltpu.make_async_copy(whole_ref.at[at], held.at[at], sems_in.at[chunk, index])
            move.start()
            arrivals.append(move)
    leaving = []

    def leave(source, target, sem):
        leaving.append(pltpu.make_async_copy(source, target, sem))
        leaving[-1].start()

    for chunk in range(chunks):
        at = pl.ds(chunk * rows, rows)
        arrivals[2 * chunk].wait()
        for target in range(n_own):
            for group in range(groups):
                column = (group * n_own + target) * own
                g_parts[target, group, at] = g_held[at, column : column + own]
        for copy in range(2):
            leave(
                g_parts.at[:, :, at],
                g_parts_ref.at[pl.ds(copy * n_own, n_own), :, at],
                sems_out.at[chunk, copy],
            )
        arrivals[2 * chunk + 1].wait()
        for target in range(n_side):
            for group in range(groups):
                block = group * n_own + (1 - side_ref[0]) * n_side + target
                column = pl.multiple_of(block * own, own)
                x_parts_ref[target, group, at] = x_held[at, pl.ds(column, own)]
    for move in leaving:
        move.wait()


def join_kernel(parts_ref, value_ref, sems):
    n_own, groups, _, own = parts_ref.shape
    moves = []
    for source in range(n_own):
        for group in range(groups):
            at = (group * n_own + source) * own
            moves.append(
                pltpu.make_async_copy(
                    parts_ref.at[source, group], value_ref.at[:, at : at + own], sems.at[source, group]
                )
            )
    for move in moves:
        move.start()
    for move in moves:
        move.wait()


def exchanged(value, devices, bit):
    return lax.ppermute(value, "seq", [(i, i ^ bit) for i in range(devices)])


def on_device(inputs, grad_out, filter_weight, filter_rates, filter_freqs, skip_gain, span_of_slot):
    rows_dev, channels = inputs.shape
    rows = rows_dev // 2
    n_basis = filter_weight.shape[0]
    devices = lax.axis_size("seq")
    position = lax.axis_index("seq")
    n_own = devices // 2
    half, rank = position // n_own, position % n_own
    own = channels // devices
    width = -(-own // LANES) * LANES
    lanes = 2 * width

    def widened(value):
        return jnp.pad(value, ((0, 0),) * (value.ndim - 1) + ((0, width - own),))

    def own_blocks(value):
        blocks = value.reshape(value.shape[0], 2, n_own, own)
        taken = lax.dynamic_index_in_dim(blocks, rank, 2, keepdims=False)
        return widened(taken).reshape(value.shape[0], lanes)

    anywhere = pl.BlockSpec(memory_space=pl.ANY)
    smem = pl.BlockSpec(memory_space=pltpu.SMEM)
    vmem = pl.BlockSpec(memory_space=pltpu.VMEM)
    small = pltpu.CompilerParams(vmem_limit_bytes=2**20)
    n_side = n_own // 2
    side = rank // n_side
    x_blocks = inputs.reshape(rows_dev, 2, n_own, own).transpose(2, 1, 0, 3)
    if own % LANES == 0:
        blocks, x_sent = pl.pallas_call(
            split_kernel,
            out_shape=(
                jax.ShapeDtypeStruct((devices, 2, rows_dev, own), BF16),
                jax.ShapeDtypeStruct((n_side, 2, rows_dev, own), BF16),
            ),
            in_specs=[smem, pl.BlockSpec(memory_space=pltpu.HBM), pl.BlockSpec(memory_space=pltpu.HBM)],
            out_specs=(anywhere, vmem),
            scratch_shapes=[
                pltpu.VMEM((rows_dev, channels), BF16),
                pltpu.VMEM((rows_dev, channels), BF16),
                pltpu.VMEM((n_own, 2, rows_dev, own), BF16),
                pltpu.SemaphoreType.DMA((4, 2)),
                pltpu.SemaphoreType.DMA((4, 2)),
            ],
            compiler_params=pltpu.CompilerParams(vmem_limit_bytes=60 * 2**20),
            name="split",
        )(side.astype(jnp.int32)[None], grad_out, inputs)
    else:
        blocks = grad_out.reshape(rows_dev, 2, n_own, own).transpose(2, 1, 0, 3)
        blocks = jnp.concatenate([blocks, blocks], 0)
        x_sent = lax.dynamic_slice_in_dim(x_blocks, (1 - side) * n_side, n_side, 0)
    received = exchanged(x_sent, devices, n_side)
    received, *others = lax.optimization_barrier(
        (received, filter_weight, filter_rates, filter_freqs, skip_gain, span_of_slot, x_blocks)
    )
    filter_weight, filter_rates, filter_freqs, skip_gain, span_of_slot, x_blocks = others
    x_kept = lax.dynamic_slice_in_dim(x_blocks, side * n_side, n_side, 0)
    x_all = jnp.stack([x_kept, received], 1)
    bit = n_side // 2
    while bit:
        x_all = x_all.reshape(2, bit, *x_all.shape[1:])
        mine = rank // bit % 2
        x_kept = lax.dynamic_index_in_dim(x_all, mine, 0, keepdims=False)
        x_sent = lax.dynamic_index_in_dim(x_all, 1 - mine, 0, keepdims=False)
        x_all = jnp.concatenate([x_kept, exchanged(x_sent, devices, bit)], 1)
        bit //= 2
    g = widened(lax.all_to_all(blocks, "seq", 0, 0, tiled=True))
    x = widened(x_all[0])
    left_g, left_x, back, spectrum, step = tables(rows, filter_rates, filter_freqs)
    g, x = lax.optimization_barrier((g, x))
    weight = own_blocks(filter_weight)
    gain = own_blocks(skip_gain[None, :])
    place = jnp.concatenate([jnp.stack([half, rank]).astype(jnp.int32), span_of_slot])
    n_spans = 2 * devices
    params = pltpu.CompilerParams(vmem_limit_bytes=24 * 2**20)
    y, states = pl.pallas_call(
        input_kernel,
        out_shape=(
            jax.ShapeDtypeStruct((n_own, 2, rows_dev, width), BF16),
            jax.ShapeDtypeStruct((devices, 2 * n_basis, lanes), F32),
        ),
        in_specs=[smem] + [vmem] * 7,
        out_specs=(anywhere, vmem),
        scratch_shapes=[
            pltpu.SMEM((n_spans,), jnp.int32),
            pltpu.VMEM((n_spans, 2 * n_basis, lanes), F32),
            pltpu.VMEM((n_spans, 2 * n_basis, lanes), F32),
            pltpu.VMEM((devices, 2 * rows, lanes), BF16),
            pltpu.VMEM((devices, 2 * rows, lanes), BF16),
            pltpu.VMEM((n_own, 2, rows_dev, width), BF16),
            pltpu.SemaphoreType.DMA((n_own,)),
        ],
        compiler_params=params,
        cost_estimate=pl.CostEstimate(flops=4*10**10, bytes_accessed=2**20, transcendentals=0),
        name="input_part",
    )(place, g, weight, gain, left_g, back, spectrum, step)
    y = lax.all_to_all(
        y[..., :own],
        "seq",
        0,
        0,
        tiled=True,
        axis_index_groups=[list(range(n_own)), list(range(n_own, devices))],
    )
    if own % LANES == 0:
        input_grad = pl.pallas_call(
            join_kernel,
            out_shape=jax.ShapeDtypeStruct((rows_dev, channels), BF16),
            in_specs=[anywhere],
            out_specs=anywhere,
            scratch_shapes=[pltpu.SemaphoreType.DMA((n_own, 2))],
            compiler_params=small,
            name="join",
        )(y)
    else:
        input_grad = y.transpose(2, 1, 0, 3).reshape(rows_dev, channels)
    wgrad = pl.pallas_call(
        weight_kernel,
        out_shape=jax.ShapeDtypeStruct((2, n_basis, width), F32),
        in_specs=[smem] + [vmem] * 6,
        out_specs=vmem,
        compiler_params=params,
        cost_estimate=pl.CostEstimate(
            flops=50 * 8 * (rows + n_basis) * rows * n_spans * lanes,
            bytes_accessed=4 * n_spans * rows * lanes,
            transcendentals=0,
        ),
        name="weight_part",
    )(place, g, states, left_g, left_x, spectrum, x)
    other = lax.ppermute(wgrad[1], "seq", [(i, i ^ n_own) for i in range(devices)])
    return input_grad, (wgrad[0] + other)[:, :own]


def solution(mesh):
    placed = (
        P(("groups", "seq"), None),
        P(("groups", "seq"), None),
        P(),
        P(),
        P(),
        P(),
        P("groups"),
    )
    return jax.shard_map(
        on_device,
        mesh=mesh,
        in_specs=placed,
        out_specs=(P(("groups", "seq"), None), P("groups", "seq")),
        check_vma=False,
    )
```

```python
import functools
import math

import jax
import jax.numpy as jnp
import numpy as np
from jax import lax
from jax.experimental import pallas as pl
from jax.experimental.pallas import tpu as pltpu
from jax.sharding import PartitionSpec as P

HIGHEST = lax.Precision.HIGHEST
F32 = jnp.float32
BF16 = jnp.bfloat16
LANES = 128


def halves(value):
    high = value.astype(BF16)
    return high, (value - high.astype(F32)).astype(BF16)


def table_halves(value):
    high = lax.reduce_precision(value, 8, 7)
    return high.astype(BF16), (value - high).astype(BF16)


def odd_frequencies(rows):
    angles = np.pi * np.outer(2 * np.arange(rows) + 1, np.arange(rows)) / (2 * rows)
    return np.cos(angles), -np.sin(angles)


def tables(rows, rates, freqs, inputs):
    cos_part, sin_part = odd_frequencies(rows)
    forward = jnp.asarray(np.concatenate([cos_part, sin_part], 0), F32)
    inverse = jnp.asarray(np.concatenate([cos_part, sin_part], 0).T / rows, F32)
    lags = jnp.arange(rows + 1).astype(F32)[None, :]
    decay = jnp.exp(-lags * rates[:, None])
    power_real = decay * jnp.cos(lags * freqs[:, None])
    power_imag = decay * jnp.sin(lags * freqs[:, None])
    to_start = jnp.concatenate([power_real[:, :rows], power_imag[:, :rows]], 0)
    to_end = jnp.concatenate([power_real[:, :0:-1], power_imag[:, :0:-1]], 0)
    left_g = jnp.concatenate(table_halves(jnp.concatenate([forward, to_start], 0)), 1)
    left_x = jnp.concatenate(table_halves(jnp.concatenate([forward, to_end], 0)), 1)
    back = jnp.concatenate(
        [inverse, power_real[:, :0:-1].T, -power_imag[:, :0:-1].T], 1
    )
    back = jnp.concatenate(table_halves(back), 0)
    basis_spectrum = jnp.dot(
        forward, power_real[:, :rows].T, precision=HIGHEST, preferred_element_type=F32
    )
    later_inputs, basis_spectrum = lax.optimization_barrier((inputs, basis_spectrum))
    step = jnp.stack([power_real[:, rows], power_imag[:, rows]], 0)[:, :, None]
    return (left_g, left_x, back, basis_spectrum, step), later_inputs


def side_by_side(ref, source, part):
    rows = ref.shape[2] // 2
    at = slice(part * rows, (part + 1) * rows)
    return jnp.concatenate([ref[source, 0, at, :], ref[source, 1, at, :]], 1)


def twice(value):
    return jnp.concatenate([value, value], 0)


def input_kernel(
    place_ref,
    g_ref,
    weight_ref,
    gain_ref,
    left_g_ref,
    back_ref,
    taps_ref,
    step_ref,
    y_ref,
    states_ref,
    sums,
    states,
    high,
    low,
    result,
    sems,
):
    n_src, _, rows_dev, width = g_ref.shape
    rows = rows_dev // 2
    n_basis, lanes = weight_ref.shape
    n_spans = 2 * n_src
    n_own = n_src // 2
    own_base = place_ref[0] * n_own
    far_base = n_own - own_base
    weight = weight_ref[...]
    taps_real, taps_imag = taps_ref[:rows], taps_ref[rows:]
    left = left_g_ref[...]
    def spread(slot, of_g):
        sums[2 * own_base + slot] = of_g[2 * rows :]
        g_real, g_imag = of_g[:rows], of_g[rows : 2 * rows]
        y_real = halves(taps_real * g_real + taps_imag * g_imag)
        y_imag = halves(taps_real * g_imag - taps_imag * g_real)
        high[slot, :rows] = y_real[0]
        high[slot, rows:] = y_imag[0]
        low[slot, :rows] = y_real[1]
        low[slot, rows:] = y_imag[1]

    waiting = []
    for slot in range(2 * n_own):
        source, part = slot // 2, slot % 2
        near = twice(side_by_side(g_ref, own_base + source, part))
        waiting.append((slot, jnp.dot(left, near, preferred_element_type=F32)))
        far = twice(side_by_side(g_ref, far_base + source, part))
        sums[2 * far_base + slot] = jnp.dot(left[2 * rows :], far, preferred_element_type=F32)
        if len(waiting) > 1:
            spread(*waiting.pop(0))
    for item in waiting:
        spread(*item)
    step_real = jnp.broadcast_to(step_ref[0], (n_basis, lanes))
    step_imag = jnp.broadcast_to(step_ref[1], (n_basis, lanes))
    state_real = jnp.zeros((n_basis, lanes), F32)
    state_imag = jnp.zeros((n_basis, lanes), F32)
    for span in range(n_spans - 1, -1, -1):
        slot = place_ref[2 + span]
        states[slot, :n_basis] = state_real
        states[slot, n_basis:] = state_imag
        if span:
            next_real = sums[slot, :n_basis] + step_real * state_real - step_imag * state_imag
            state_imag = sums[slot, n_basis:] + step_real * state_imag + step_imag * state_real
            state_real = next_real
    gain = gain_ref[...]
    both_weight = twice(weight)
    leaving = []
    def finish(slot, by_high, by_low):
        source, part = slot // 2, slot % 2
        own = side_by_side(g_ref, own_base + source, part).astype(F32)
        value = ((by_high[:rows] + by_high[rows:]) + by_low + gain * own).astype(BF16)
        at = slice(part * rows, (part + 1) * rows)
        result[source, 0, at, :] = value[:, :width]
        result[source, 1, at, :] = value[:, width:]
        if part:
            leaving.append(
                pltpu.make_async_copy(result.at[source], y_ref.at[source], sems.at[source])
            )
            leaving[-1].start()

    waiting = []
    for slot in range(2 * n_own):
        state = states[2 * own_base + slot]
        states_ref[slot] = state
        far = halves(both_weight * state)
        both_high = jnp.concatenate([high[slot], far[0]], 0)
        both_low = jnp.concatenate([low[slot], far[1]], 0)
        by_high = jnp.dot(back_ref[...], both_high, preferred_element_type=F32)
        by_low = jnp.dot(back_ref[:rows], both_low, preferred_element_type=F32)
        waiting.append((slot, by_high, by_low))
        if len(waiting) > 1:
            finish(*waiting.pop(0))
    for item in waiting:
        finish(*item)
    for move in leaving:
        move.wait()


def weight_kernel(place_ref, g_ref, states_ref, left_g_ref, left_x_ref, spectrum_ref, *refs):
    x_refs, wgrad_ref = refs[:-1], refs[-1]
    n_own = len(x_refs)
    rows_dev, width = g_ref.shape[2:]
    rows = rows_dev // 2
    n_basis, lanes = states_ref.shape[1] // 2, states_ref.shape[2]
    half, own = place_ref[0], place_ref[1]
    left_g, left_x = left_g_ref[: 2 * rows], left_x_ref[...]
    cross_real = jnp.zeros((rows, lanes), F32)
    cross_imag = jnp.zeros((rows, lanes), F32)
    total = jnp.zeros((n_basis, lanes), F32)
    for offset, x_ref in enumerate(x_refs):
        source = own ^ offset
        for part in range(2):
            at = slice(part * rows, (part + 1) * rows)
            g = twice(side_by_side(g_ref, half * n_own + source, part))
            x = twice(jnp.concatenate([x_ref[0, at, :], x_ref[1, at, :]], 1))
            of_g = jnp.dot(left_g, g, preferred_element_type=F32)
            of_x = jnp.dot(left_x, x, preferred_element_type=F32)
            g_real, g_imag = of_g[:rows], of_g[rows:]
            x_real, x_imag = of_x[:rows], of_x[rows : 2 * rows]
            cross_real = cross_real + (x_real * g_real + x_imag * g_imag)
            cross_imag = cross_imag + (x_real * g_imag - x_imag * g_real)
            product = states_ref[2 * source + part] * of_x[2 * rows :]
            total = total + (product[:n_basis] - product[n_basis:])
    total = total + lax.dot_general(
        spectrum_ref[...],
        jnp.concatenate([cross_real, cross_imag], 0) * (1.0 / rows),
        (((0,), (0,)), ((), ())),
        precision=HIGHEST,
        preferred_element_type=F32,
    )
    for block in range(2):
        wgrad_ref[half ^ block] = total[:, block * width : (block + 1) * width]


def split_kernel(value_ref, parts_ref, held, parts, sems_in, sems_out):
    n_own, groups, rows_dev, own = parts.shape
    chunks = sems_in.shape[0]
    rows = rows_dev // chunks
    copies = parts_ref.shape[0] // n_own
    arrivals = []
    for chunk in range(chunks):
        at = pl.ds(chunk * rows, rows)
        arrivals.append(pltpu.make_async_copy(value_ref.at[at], held.at[at], sems_in.at[chunk]))
        arrivals[-1].start()
    leaving = []
    for chunk in range(chunks):
        at = pl.ds(chunk * rows, rows)
        arrivals[chunk].wait()
        for target in range(n_own):
            for group in range(groups):
                column = (group * n_own + target) * own
                parts[target, group, at] = held[at, column : column + own]
        for copy in range(copies):
            leaving.append(
                pltpu.make_async_copy(
                    parts.at[:, :, at],
                    parts_ref.at[pl.ds(copy * n_own, n_own), :, at],
                    sems_out.at[chunk, copy],
                )
            )
            leaving[-1].start()
    for move in leaving:
        move.wait()


def join_kernel(parts_ref, value_ref, held, sems):
    n_own, groups, rows_dev, own = parts_ref.shape
    chunks = sems.shape[0]
    rows = rows_dev // chunks
    leaving = []
    for chunk in range(chunks):
        at = pl.ds(chunk * rows, rows)
        for source in range(n_own):
            for group in range(groups):
                column = (group * n_own + source) * own
                held[at, column : column + own] = parts_ref[source, group, at]
        leaving.append(pltpu.make_async_copy(held.at[at], value_ref.at[at], sems.at[chunk]))
        leaving[-1].start()
    for move in leaving:
        move.wait()


def on_device(inputs, grad_out, filter_weight, filter_rates, filter_freqs, skip_gain, span_of_slot):
    rows_dev, channels = inputs.shape
    rows = rows_dev // 2
    n_basis = filter_weight.shape[0]
    devices = lax.axis_size("seq")
    position = lax.axis_index("seq")
    n_own = devices // 2
    half, rank = position // n_own, position % n_own
    own = channels // devices
    width = -(-own // LANES) * LANES
    lanes = 2 * width

    def widened(value):
        return jnp.pad(value, ((0, 0),) * (value.ndim - 1) + ((0, width - own),))

    def own_blocks(value):
        blocks = value.reshape(value.shape[0], 2, n_own, own)
        taken = lax.dynamic_index_in_dim(blocks, rank, 2, keepdims=False)
        return widened(taken).reshape(value.shape[0], lanes)

    anywhere = pl.BlockSpec(memory_space=pl.ANY)
    small = pltpu.CompilerParams(vmem_limit_bytes=2**20)
    if own % LANES == 0:
        blocks = pl.pallas_call(
            split_kernel,
            out_shape=jax.ShapeDtypeStruct((devices, 2, rows_dev, own), BF16),
            in_specs=[pl.BlockSpec(memory_space=pltpu.HBM)],
            out_specs=anywhere,
            scratch_shapes=[
                pltpu.VMEM((rows_dev, channels), BF16),
                pltpu.VMEM((n_own, 2, rows_dev, own), BF16),
                pltpu.SemaphoreType.DMA((4,)),
                pltpu.SemaphoreType.DMA((4, 2)),
            ],
            compiler_params=pltpu.CompilerParams(vmem_limit_bytes=60 * 2**20),
            name="split",
        )(grad_out)
    else:
        blocks = grad_out.reshape(rows_dev, 2, n_own, own).transpose(2, 1, 0, 3)
        blocks = jnp.concatenate([blocks, blocks], 0)
    g = widened(lax.all_to_all(blocks, "seq", 0, 0, tiled=True))
    made, later_inputs = tables(rows, filter_rates, filter_freqs, inputs)
    left_g, left_x, back, spectrum, step = made
    x_blocks = later_inputs.reshape(rows_dev, 2, n_own, own)
    x_parts = []
    for offset in range(n_own):
        part = lax.dynamic_index_in_dim(x_blocks, rank ^ offset, 2, keepdims=False)
        part = part.transpose(1, 0, 2)
        if offset:
            part = lax.ppermute(part, "seq", [(i, i ^ offset) for i in range(devices)])
        x_parts.append(widened(part))
    weight = own_blocks(filter_weight)
    gain = own_blocks(skip_gain[None, :])
    slots = jnp.arange(2 * devices, dtype=jnp.int32)
    slot_of_span = jnp.sum(
        jnp.where(span_of_slot[None, :] == slots[:, None], slots[None, :], 0), 1, dtype=jnp.int32
    )
    place = jnp.concatenate([jnp.stack([half, rank]).astype(jnp.int32), slot_of_span])
    n_spans = 2 * devices
    taps = jnp.dot(spectrum, weight, precision=HIGHEST, preferred_element_type=F32)
    smem = pl.BlockSpec(memory_space=pltpu.SMEM)
    vmem = pl.BlockSpec(memory_space=pltpu.VMEM)
    params = pltpu.CompilerParams(vmem_limit_bytes=24 * 2**20)
    y, states = pl.pallas_call(
        input_kernel,
        out_shape=(
            jax.ShapeDtypeStruct((n_own, 2, rows_dev, width), BF16),
            jax.ShapeDtypeStruct((devices, 2 * n_basis, lanes), F32),
        ),
        in_specs=[smem] + [vmem] * 7,
        out_specs=(anywhere, vmem),
        scratch_shapes=[
            pltpu.VMEM((n_spans, 2 * n_basis, lanes), F32),
            pltpu.VMEM((n_spans, 2 * n_basis, lanes), F32),
            pltpu.VMEM((devices, 2 * rows, lanes), BF16),
            pltpu.VMEM((devices, 2 * rows, lanes), BF16),
            pltpu.VMEM((n_own, 2, rows_dev, width), BF16),
            pltpu.SemaphoreType.DMA((n_own,)),
        ],
        compiler_params=params,
        cost_estimate=pl.CostEstimate(flops=4*10**10, bytes_accessed=2**20, transcendentals=0),
        name="input_part",
    )(place, g, weight, gain, left_g, back, taps, step)
    y = lax.all_to_all(
        y[..., :own],
        "seq",
        0,
        0,
        tiled=True,
        axis_index_groups=[list(range(n_own)), list(range(n_own, devices))],
    )
    if own % LANES == 0:
        input_grad = pl.pallas_call(
            join_kernel,
            out_shape=jax.ShapeDtypeStruct((rows_dev, channels), BF16),
            in_specs=[vmem],
            out_specs=anywhere,
            scratch_shapes=[
                pltpu.VMEM((rows_dev, channels), BF16),
                pltpu.SemaphoreType.DMA((4,)),
            ],
            compiler_params=small,
            name="join",
        )(y)
    else:
        input_grad = y.transpose(2, 1, 0, 3).reshape(rows_dev, channels)
    wgrad = pl.pallas_call(
        weight_kernel,
        out_shape=jax.ShapeDtypeStruct((2, n_basis, width), F32),
        in_specs=[smem] + [vmem] * (5 + n_own),
        out_specs=vmem,
        compiler_params=params,
        cost_estimate=pl.CostEstimate(
            flops=50 * 8 * (rows + n_basis) * rows * n_spans * lanes,
            bytes_accessed=4 * n_spans * rows * lanes,
            transcendentals=0,
        ),
        name="weight_part",
    )(place, g, states, left_g, left_x, spectrum, *x_parts)
    other = lax.ppermute(wgrad[1], "seq", [(i, i ^ n_own) for i in range(devices)])
    return input_grad, (wgrad[0] + other)[:, :own]


def solution(mesh):
    placed = (
        P(("groups", "seq"), None),
        P(("groups", "seq"), None),
        P(),
        P(),
        P(),
        P(),
        P("groups"),
    )
    return jax.shard_map(
        on_device,
        mesh=mesh,
        in_specs=placed,
        out_specs=(P(("groups", "seq"), None), P("groups", "seq")),
        check_vma=False,
    )
```

```python
import functools
import math

import jax
import jax.numpy as jnp
import numpy as np
from jax import lax
from jax.experimental import pallas as pl
from jax.experimental.pallas import tpu as pltpu
from jax.sharding import PartitionSpec as P

HIGHEST = lax.Precision.HIGHEST
F32 = jnp.float32
BF16 = jnp.bfloat16
LANES = 128


def halves(value):
    high = value.astype(BF16)
    return high, (value - high.astype(F32)).astype(BF16)


def table_halves(value):
    high = lax.reduce_precision(value, 8, 7)
    return high.astype(BF16), (value - high).astype(BF16)


def odd_frequencies(rows):
    angles = np.pi * np.outer(2 * np.arange(rows) + 1, np.arange(rows)) / (2 * rows)
    return np.cos(angles), -np.sin(angles)


def tables(rows, rates, freqs, inputs):
    cos_part, sin_part = odd_frequencies(rows)
    forward = jnp.asarray(np.concatenate([cos_part, sin_part], 0), F32)
    inverse = jnp.asarray(np.concatenate([cos_part, sin_part], 0).T / rows, F32)
    lags = jnp.arange(rows + 1).astype(F32)[None, :]
    decay = jnp.exp(-lags * rates[:, None])
    power_real = decay * jnp.cos(lags * freqs[:, None])
    power_imag = decay * jnp.sin(lags * freqs[:, None])
    to_start = jnp.concatenate([power_real[:, :rows], power_imag[:, :rows]], 0)
    to_end = jnp.concatenate([power_real[:, :0:-1], power_imag[:, :0:-1]], 0)
    left_g = jnp.concatenate(table_halves(jnp.concatenate([forward, to_start], 0)), 1)
    left_x = jnp.concatenate(table_halves(jnp.concatenate([forward, to_end], 0)), 1)
    back = jnp.concatenate(
        [inverse, power_real[:, :0:-1].T, -power_imag[:, :0:-1].T], 1
    )
    back_high, back_low = table_halves(back)
    back = jnp.concatenate([back_high, back_low], 0)
    far = jnp.concatenate([back_high[:, 2 * rows :]] * 2 + [back_low[:, 2 * rows :]], 1)
    basis_spectrum = jnp.dot(
        forward, power_real[:, :rows].T, precision=HIGHEST, preferred_element_type=F32
    )
    step = jnp.stack([power_real[:, rows], power_imag[:, rows]], 0)[:, :, None]
    later_inputs, left_g, back, far, basis_spectrum = lax.optimization_barrier(
        (inputs, left_g, back, far, basis_spectrum)
    )
    return (left_g, left_x, back, far, basis_spectrum, step), later_inputs


def side_by_side(ref, source, part):
    rows = ref.shape[2] // 2
    at = slice(part * rows, (part + 1) * rows)
    return jnp.concatenate([ref[source, 0, at, :], ref[source, 1, at, :]], 1)


def twice(value):
    return jnp.concatenate([value, value], 0)


def input_kernel(
    place_ref,
    g_ref,
    weight_ref,
    gain_ref,
    left_g_ref,
    back_ref,
    far_ref,
    taps_ref,
    step_ref,
    y_ref,
    states_ref,
    sums,
    states,
    high,
    low,
    nears,
    result,
    sems,
):
    n_src, _, rows_dev, width = g_ref.shape
    rows = rows_dev // 2
    n_basis, lanes = weight_ref.shape
    n_spans = 2 * n_src
    n_own = n_src // 2
    own_base = place_ref[0] * n_own
    far_base = n_own - own_base
    weight = weight_ref[...]
    taps_real, taps_imag = taps_ref[:rows], taps_ref[rows:]
    left = left_g_ref[...]
    def spread(slot, of_g):
        sums[2 * own_base + slot] = of_g[2 * rows :]
        g_real, g_imag = of_g[:rows], of_g[rows : 2 * rows]
        y_real = halves(taps_real * g_real + taps_imag * g_imag)
        y_imag = halves(taps_real * g_imag - taps_imag * g_real)
        high[slot, :rows] = y_real[0]
        high[slot, rows:] = y_imag[0]
        low[slot, :rows] = y_real[1]
        low[slot, rows:] = y_imag[1]

    waiting = []
    for slot in range(2 * n_own):
        source, part = slot // 2, slot % 2
        near = twice(side_by_side(g_ref, own_base + source, part))
        waiting.append((slot, jnp.dot(left, near, preferred_element_type=F32)))
        far = twice(side_by_side(g_ref, far_base + source, part))
        sums[2 * far_base + slot] = jnp.dot(left[2 * rows :], far, preferred_element_type=F32)
        if len(waiting) > 1:
            spread(*waiting.pop(0))
    for item in waiting:
        spread(*item)
    step_real = jnp.broadcast_to(step_ref[0], (n_basis, lanes))
    step_imag = jnp.broadcast_to(step_ref[1], (n_basis, lanes))
    state_real = jnp.zeros((n_basis, lanes), F32)
    state_imag = jnp.zeros((n_basis, lanes), F32)
    gain = gain_ref[...]
    both_weight = twice(weight)
    leaving = []

    def descend(span, state_real, state_imag):
        slot = place_ref[2 + span]
        states[slot, :n_basis] = state_real
        states[slot, n_basis:] = state_imag
        if not span:
            return state_real, state_imag
        return (
            sums[slot, :n_basis] + step_real * state_real - step_imag * state_imag,
            sums[slot, n_basis:] + step_real * state_imag + step_imag * state_real,
        )

    def keep(slot, by_high, by_low):
        own = side_by_side(g_ref, own_base + slot // 2, slot % 2).astype(F32)
        nears[slot] = (by_high[:rows] + by_high[rows:]) + by_low + gain * own

    waiting = []
    for slot in range(2 * n_own):
        by_high = jnp.dot(back_ref[:, : 2 * rows], high[slot], preferred_element_type=F32)
        by_low = jnp.dot(back_ref[:rows, : 2 * rows], low[slot], preferred_element_type=F32)
        waiting.append((slot, by_high, by_low))
        for span in range(n_spans - 1 - 2 * slot, n_spans - 3 - 2 * slot, -1):
            state_real, state_imag = descend(span, state_real, state_imag)
        if len(waiting) > 1:
            keep(*waiting.pop(0))
    for item in waiting:
        keep(*item)

    def finish(slot, far):
        source, part = slot // 2, slot % 2
        value = (nears[slot] + far).astype(BF16)
        at = slice(part * rows, (part + 1) * rows)
        result[source, 0, at, :] = value[:, :width]
        result[source, 1, at, :] = value[:, width:]
        if part:
            leaving.append(
                pltpu.make_async_copy(result.at[source], y_ref.at[source], sems.at[source])
            )
            leaving[-1].start()

    waiting = []
    for slot in range(2 * n_own):
        state = states[2 * own_base + slot]
        states_ref[slot] = state
        far_high, far_low = halves(both_weight * state)
        far = jnp.dot(
            far_ref[...],
            jnp.concatenate([far_high, far_low, far_high], 0),
            preferred_element_type=F32,
        )
        waiting.append((slot, far))
        if len(waiting) > 1:
            finish(*waiting.pop(0))
    for item in waiting:
        finish(*item)
    for move in leaving:
        move.wait()


def weight_kernel(place_ref, g_ref, states_ref, left_g_ref, left_x_ref, spectrum_ref, *refs):
    x_refs, wgrad_ref = refs[:-1], refs[-1]
    n_own = len(x_refs)
    rows_dev, width = g_ref.shape[2:]
    rows = rows_dev // 2
    n_basis, lanes = states_ref.shape[1] // 2, states_ref.shape[2]
    half, own = place_ref[0], place_ref[1]
    left_g, left_x = left_g_ref[: 2 * rows], left_x_ref[...]
    cross_real = jnp.zeros((rows, lanes), F32)
    cross_imag = jnp.zeros((rows, lanes), F32)
    total = jnp.zeros((n_basis, lanes), F32)
    for offset, x_ref in enumerate(x_refs):
        source = own ^ offset
        for part in range(2):
            at = slice(part * rows, (part + 1) * rows)
            g = twice(side_by_side(g_ref, half * n_own + source, part))
            x = twice(jnp.concatenate([x_ref[0, at, :], x_ref[1, at, :]], 1))
            of_g = jnp.dot(left_g, g, preferred_element_type=F32)
            of_x = jnp.dot(left_x, x, preferred_element_type=F32)
            g_real, g_imag = of_g[:rows], of_g[rows:]
            x_real, x_imag = of_x[:rows], of_x[rows : 2 * rows]
            cross_real = cross_real + (x_real * g_real + x_imag * g_imag)
            cross_imag = cross_imag + (x_real * g_imag - x_imag * g_real)
            product = states_ref[2 * source + part] * of_x[2 * rows :]
            total = total + (product[:n_basis] - product[n_basis:])
    total = total + lax.dot_general(
        spectrum_ref[...],
        jnp.concatenate([cross_real, cross_imag], 0) * (1.0 / rows),
        (((0,), (0,)), ((), ())),
        precision=HIGHEST,
        preferred_element_type=F32,
    )
    for block in range(2):
        wgrad_ref[half ^ block] = total[:, block * width : (block + 1) * width]


def split_kernel(value_ref, parts_ref, held, parts, sems_in, sems_out):
    n_own, groups, rows_dev, own = parts.shape
    chunks = sems_in.shape[0]
    rows = rows_dev // chunks
    copies = parts_ref.shape[0] // n_own
    arrivals = []
    for chunk in range(chunks):
        at = pl.ds(chunk * rows, rows)
        arrivals.append(pltpu.make_async_copy(value_ref.at[at], held.at[at], sems_in.at[chunk]))
        arrivals[-1].start()
    leaving = []
    for chunk in range(chunks):
        at = pl.ds(chunk * rows, rows)
        arrivals[chunk].wait()
        for target in range(n_own):
            for group in range(groups):
                column = (group * n_own + target) * own
                parts[target, group, at] = held[at, column : column + own]
        for copy in range(copies):
            leaving.append(
                pltpu.make_async_copy(
                    parts.at[:, :, at],
                    parts_ref.at[pl.ds(copy * n_own, n_own), :, at],
                    sems_out.at[chunk, copy],
                )
            )
            leaving[-1].start()
    for move in leaving:
        move.wait()


def join_kernel(parts_ref, value_ref, held, sems):
    n_own, groups, rows_dev, own = parts_ref.shape
    chunks = sems.shape[0]
    rows = rows_dev // chunks
    leaving = []
    for chunk in range(chunks):
        at = pl.ds(chunk * rows, rows)
        for source in range(n_own):
            for group in range(groups):
                column = (group * n_own + source) * own
                held[at, column : column + own] = parts_ref[source, group, at]
        leaving.append(pltpu.make_async_copy(held.at[at], value_ref.at[at], sems.at[chunk]))
        leaving[-1].start()
    for move in leaving:
        move.wait()


def on_device(inputs, grad_out, filter_weight, filter_rates, filter_freqs, skip_gain, span_of_slot):
    rows_dev, channels = inputs.shape
    rows = rows_dev // 2
    n_basis = filter_weight.shape[0]
    devices = lax.axis_size("seq")
    position = lax.axis_index("seq")
    n_own = devices // 2
    half, rank = position // n_own, position % n_own
    own = channels // devices
    width = -(-own // LANES) * LANES
    lanes = 2 * width

    def widened(value):
        return jnp.pad(value, ((0, 0),) * (value.ndim - 1) + ((0, width - own),))

    def own_blocks(value):
        blocks = value.reshape(value.shape[0], 2, n_own, own)
        taken = lax.dynamic_index_in_dim(blocks, rank, 2, keepdims=False)
        return widened(taken).reshape(value.shape[0], lanes)

    anywhere = pl.BlockSpec(memory_space=pl.ANY)
    small = pltpu.CompilerParams(vmem_limit_bytes=2**20)
    if own % LANES == 0:
        blocks = pl.pallas_call(
            split_kernel,
            out_shape=jax.ShapeDtypeStruct((devices, 2, rows_dev, own), BF16),
            in_specs=[pl.BlockSpec(memory_space=pltpu.HBM)],
            out_specs=anywhere,
            scratch_shapes=[
                pltpu.VMEM((rows_dev, channels), BF16),
                pltpu.VMEM((n_own, 2, rows_dev, own), BF16),
                pltpu.SemaphoreType.DMA((4,)),
                pltpu.SemaphoreType.DMA((4, 2)),
            ],
            compiler_params=pltpu.CompilerParams(vmem_limit_bytes=60 * 2**20),
            name="split",
        )(grad_out)
    else:
        blocks = grad_out.reshape(rows_dev, 2, n_own, own).transpose(2, 1, 0, 3)
        blocks = jnp.concatenate([blocks, blocks], 0)
    g = widened(lax.all_to_all(blocks, "seq", 0, 0, tiled=True))
    made, later_inputs = tables(rows, filter_rates, filter_freqs, inputs)
    left_g, left_x, back, far, spectrum, step = made
    x_blocks = later_inputs.reshape(rows_dev, 2, n_own, own)
    x_parts = []
    for offset in range(n_own):
        part = lax.dynamic_index_in_dim(x_blocks, rank ^ offset, 2, keepdims=False)
        part = part.transpose(1, 0, 2)
        if offset:
            part = lax.ppermute(part, "seq", [(i, i ^ offset) for i in range(devices)])
        x_parts.append(widened(part))
    weight = own_blocks(filter_weight)
    gain = own_blocks(skip_gain[None, :])
    slots = jnp.arange(2 * devices, dtype=jnp.int32)
    slot_of_span = jnp.sum(
        jnp.where(span_of_slot[None, :] == slots[:, None], slots[None, :], 0), 1, dtype=jnp.int32
    )
    place = jnp.concatenate([jnp.stack([half, rank]).astype(jnp.int32), slot_of_span])
    n_spans = 2 * devices
    taps = jnp.dot(spectrum, weight, precision=HIGHEST, preferred_element_type=F32)
    smem = pl.BlockSpec(memory_space=pltpu.SMEM)
    vmem = pl.BlockSpec(memory_space=pltpu.VMEM)
    params = pltpu.CompilerParams(vmem_limit_bytes=24 * 2**20)
    y, states = pl.pallas_call(
        input_kernel,
        out_shape=(
            jax.ShapeDtypeStruct((n_own, 2, rows_dev, width), BF16),
            jax.ShapeDtypeStruct((devices, 2 * n_basis, lanes), F32),
        ),
        in_specs=[smem] + [vmem] * 8,
        out_specs=(anywhere, vmem),
        scratch_shapes=[
            pltpu.VMEM((n_spans, 2 * n_basis, lanes), F32),
            pltpu.VMEM((n_spans, 2 * n_basis, lanes), F32),
            pltpu.VMEM((devices, 2 * rows, lanes), BF16),
            pltpu.VMEM((devices, 2 * rows, lanes), BF16),
            pltpu.VMEM((devices, rows, lanes), F32),
            pltpu.VMEM((n_own, 2, rows_dev, width), BF16),
            pltpu.SemaphoreType.DMA((n_own,)),
        ],
        compiler_params=params,
        cost_estimate=pl.CostEstimate(flops=4*10**10, bytes_accessed=2**20, transcendentals=0),
        name="input_part",
    )(place, g, weight, gain, left_g, back, far, taps, step)
    y = lax.all_to_all(
        y[..., :own],
        "seq",
        0,
        0,
        tiled=True,
        axis_index_groups=[list(range(n_own)), list(range(n_own, devices))],
    )
    if own % LANES == 0:
        input_grad = pl.pallas_call(
            join_kernel,
            out_shape=jax.ShapeDtypeStruct((rows_dev, channels), BF16),
            in_specs=[vmem],
            out_specs=anywhere,
            scratch_shapes=[
                pltpu.VMEM((rows_dev, channels), BF16),
                pltpu.SemaphoreType.DMA((4,)),
            ],
            compiler_params=small,
            name="join",
        )(y)
    else:
        input_grad = y.transpose(2, 1, 0, 3).reshape(rows_dev, channels)
    wgrad = pl.pallas_call(
        weight_kernel,
        out_shape=jax.ShapeDtypeStruct((2, n_basis, width), F32),
        in_specs=[smem] + [vmem] * (5 + n_own),
        out_specs=vmem,
        compiler_params=params,
        cost_estimate=pl.CostEstimate(
            flops=50 * 8 * (rows + n_basis) * rows * n_spans * lanes,
            bytes_accessed=4 * n_spans * rows * lanes,
            transcendentals=0,
        ),
        name="weight_part",
    )(place, g, states, left_g, left_x, spectrum, *x_parts)
    other = lax.ppermute(wgrad[1], "seq", [(i, i ^ n_own) for i in range(devices)])
    return input_grad, (wgrad[0] + other)[:, :own]


def solution(mesh):
    placed = (
        P(("groups", "seq"), None),
        P(("groups", "seq"), None),
        P(),
        P(),
        P(),
        P(),
        P("groups"),
    )
    return jax.shard_map(
        on_device,
        mesh=mesh,
        in_specs=placed,
        out_specs=(P(("groups", "seq"), None), P("groups", "seq")),
        check_vma=False,
    )
```
